512 devices in a mesh: expert: 32 (over y, x), tensor: 16 (over z, core).
Axes of the slice: x: 4, y: 8, z: 8, core: 2. Of those that a mesh axis runs over, the one named last changes fastest.
Arguments:
- residual: bfloat16 [2048, 7168], P('expert', 'tensor'), may hold values from -40 to 40
- attn_parts: bfloat16 [16, 2048, 7168], P('tensor', 'expert'), may hold values from -2 to 2
- norm_gain: bfloat16 [7168], P('tensor'), may hold values from 0.099609375 to 1.8984375
- routes: int32 [2048, 8], P('expert'), may hold values from 0 to 31, all different within a row; in each aligned block of 64 rows (0 to 63, 64 to 127, ...) at most 24 rows name the same one
- route_weights: float32 [2048, 8], P('expert'), may hold values from 0.05 to 0.6
- w_gate: bfloat16 [32, 7168, 2048], P('expert', None, 'tensor'), may hold values from -0.06023809 to 0.06023809
- w_gate_q: bfloat16 [32, 7168, 2048], P('expert', None, 'tensor'), may hold values from -0.09567226 to 0.09567226
Outputs:
- token_error: float32 [2048], P('expert')
- expert_error: float32 [32], P('expert')
- hess_diag: float32 [32, 7168], P('expert', 'tensor')
The draws below stay inside these ranges and needn't reach their ends.
Inputs may be any that keep to these rules, and one draw needn't show every extreme that they name: `routes`: no expert is named by more than 24 of the rows of one device, and in every draw some expert is named by exactly 24 of them; the 8 experts of a token are distinct; every expert is named by some token.
All inputs are finite; a program needn't handle non-finite values.
Results may differ from the reference program's by a relative error of at most 0.0023.
Values may be sent and summed in bfloat16 or wider, within the bound.
A program may use at most 64 MiB of HBM per device.

```python
import math
import jax
import jax.numpy as jnp
import numpy as np
from jax import lax

D = 7168
FF = 2048
QGROUP = 128
TOK_DEV = 64
TOKENS = 2048
EXPERTS = 32
TOPK = 8
CAP = 24
N_EXPERT = 32
N_TENSOR = 16


def weight_pair(key):
    base_key = jax.random.fold_in(key, 7301)
    weight_scale = 1.0 / math.sqrt(D)

    def one_expert(expert_id):
        expert_key = jax.random.fold_in(base_key, expert_id)
        key_list = jax.random.split(expert_key, 4)
        base_values = jnp.clip(jax.random.normal(key_list[0], (D, FF), jnp.float32), -5.0, 5.0)
        group_scale = jnp.exp(jax.random.uniform(key_list[1], (D // QGROUP, FF), jnp.float32, math.log(0.1), 0.0))
        group_scale = jnp.repeat(group_scale, QGROUP, axis=0)
        column_scale = jnp.exp(jax.random.uniform(key_list[2], (1, FF), jnp.float32, math.log(0.3), math.log(3.0)))
        noise_values = jax.random.uniform(key_list[3], (D, FF), jnp.float32, -1.0, 1.0)
        full_values = base_values * weight_scale
        quant_values = full_values + weight_scale * group_scale * column_scale * noise_values
        return (full_values.astype(jnp.bfloat16), quant_values.astype(jnp.bfloat16))
    return lax.map(one_expert, jnp.arange(EXPERTS, dtype=jnp.int32))


def draw_w_gate(key, part):
    return weight_pair(key)[0]


def draw_w_gate_q(key, part):
    return weight_pair(key)[1]


def draw_residual(key, part):
    key_list = jax.random.split(jax.random.fold_in(key, 4409), 2)
    column = jnp.arange(D, dtype=jnp.float32)[None, :] / (D - 1)
    roughness = jnp.exp(jax.random.uniform(key_list[1], (TOKENS, D), jnp.float32, math.log(0.5), math.log(2.0)))
    ramp_scale = jnp.sqrt(1.0 + 2.0 * column)
    base_values = jnp.clip(jax.random.normal(key_list[0], (TOKENS, D), jnp.float32), -5.0, 5.0)
    return jnp.clip(base_values * ramp_scale * roughness, -40.0, 40.0).astype(jnp.bfloat16)


def spiked(entries, key, source, target, shards_of, factor):
    owner, partner = [(jnp.arange(entries.shape[axis_at]) // (entries.shape[axis_at] // shards_of)).reshape([-1 if axis == axis_at else 1 for axis in range(entries.ndim)]) for axis_at in (source, target)]
    chosen = jax.random.permutation(key, shards_of)[partner]
    strong = (owner == chosen) | (owner == (partner + shards_of // 2) % shards_of)
    return jnp.where(strong, factor * entries, entries)


def block_scale(key, dims, pieces, smallest, largest):
    gain, own = 1.0, jax.random.fold_in(key, 6)
    for dim, parts in pieces:
        steps = jnp.exp(jax.random.uniform(jax.random.fold_in(own, dim), (parts,), jnp.float32, smallest / len(pieces), largest / len(pieces)))
        gain = gain * jnp.repeat(steps, dims[dim] // parts).reshape([-1 if axis == dim else 1 for axis in range(len(dims))])
    return gain


def shared_out(own_key, own, number, rows, count, top, limit, slope):
    sequence = jax.random.permutation(own_key, count)
    heavy_load, common = shares(count, rows * top, limit, slope, True), shares(count, rows * top, limit, slope, False)
    places = jnp.arange(count)

    def named(tallies, rotation):
        used = int((tallies > 0).sum())
        fixed = max(1, used // 4)
        shifted = fixed + (places - fixed + rotation * (used - fixed)) % max(1, count - fixed)
        return jnp.zeros((count,), jnp.int32).at[sequence[jnp.where(places < fixed, places, shifted)]].set(jnp.asarray(tallies, jnp.int32))

    tallies = jnp.where(number % 4 == 0, named(heavy_load, number // 4), named(common, number - number // 4 - 1))
    mixed = jax.random.permutation(jax.random.fold_in(own, 3), count)
    source_of, taker = mixed[0:count // 2 * 2:2], mixed[1:count // 2 * 2:2]
    slack = jnp.minimum(tallies[source_of] - 1, limit - tallies[taker]) // 2
    slack = jnp.where((source_of == sequence[0]) | (taker == sequence[0]) | (tallies[taker] == 0), 0, jnp.maximum(slack, 0))
    shifted = jax.random.randint(jax.random.fold_in(own, 4), (count // 2,), 0, 1 << 20) % (slack + 1)
    tallies = tallies.at[source_of].add(-shifted).at[taker].add(shifted)
    labels = jnp.searchsorted(jnp.cumsum(tallies), jnp.arange(rows * top), side="right").astype(jnp.int32)
    table = labels.reshape(top, rows).T
    table = table[jax.random.permutation(jax.random.fold_in(own, 1), rows)]
    rotation = jax.random.randint(jax.random.fold_in(own, 2), (rows, 1), 0, top)
    return jnp.take_along_axis(table, (jnp.arange(top)[None, :] + rotation) % top, axis=1)


def shares(number_of, total, reach, slope, full):
    portions = [(1 << 20) // math.isqrt(rank ** slope) + 1 for rank in range(1, number_of + 1)]
    largest = reach if full else min(reach, max(-(-total // number_of), total * portions[0] // sum(portions)))
    least = 1 if total - largest >= number_of - 1 else 0
    given, rest = [largest] + [least] * (number_of - 1), total - largest - least * (number_of - 1)
    while rest > 0:
        movable = [i for i in range(1, number_of) if given[i] < largest] or [i for i in range(1, number_of) if given[i] < reach]
        whole, left = sum([portions[i] for i in movable]), rest
        for i in movable:
            more = min(reach - given[i], max(1, left * portions[i] // whole), rest)
            given[i] = given[i] + more
            rest = rest - more
    return np.array(given)


def noise_with(key, dims, deviation, most, shards, heavy, kind=jnp.bfloat16):
    values = deviation * jax.random.normal(key, dims, jnp.float32)
    if shards:
        values = values * block_scale(key, dims, shards, -0.22, 0.18)
    return jnp.clip(spiked(values, jax.random.fold_in(key, 3), *heavy), -most, most).astype(kind)


def setup_inputs(seed: int = 0) -> dict:
    seeds = jax.random.split(jax.random.key(seed), 8)
    residual = draw_residual(jax.random.fold_in(seeds[7], 71), 0)
    attn_parts = noise_with(seeds[1], (N_TENSOR, TOKENS, D), 0.25, 2.0, ((0, 16), (1, 32)), (0, 2, 16, 2.0))
    norm_gain = jnp.clip(1.0 + 0.18 * jax.random.normal(seeds[2], (D,), jnp.float32), 0.099609375, 1.8984375).astype(jnp.bfloat16)
    routes_keys = jax.random.split(jax.random.fold_in(seeds[3], 1), TOKENS // TOK_DEV)
    routes_turns = jax.random.permutation(jax.random.fold_in(seeds[3], 3), TOKENS // TOK_DEV)
    routes = jax.vmap(lambda own, number: shared_out(jax.random.fold_in(seeds[3], 2), own, number, TOK_DEV, EXPERTS, TOPK, CAP, 2))(routes_keys, routes_turns).reshape((TOKENS, TOPK))
    route_weights = jnp.clip(0.05 + 0.55 * jax.random.uniform(seeds[4], (TOKENS, TOPK), jnp.float32) ** block_scale(seeds[4], (TOKENS, TOPK), ((0, 32),), -0.2, 0.2), 0.05, 0.6)
    w_gate = draw_w_gate(jax.random.fold_in(seeds[7], 71), 0)
    w_gate_q = draw_w_gate_q(jax.random.fold_in(seeds[7], 71), 0)
    return {"residual": residual, "attn_parts": attn_parts, "norm_gain": norm_gain, "routes": routes, "route_weights": route_weights, "w_gate": w_gate, "w_gate_q": w_gate_q}


epsilon = 1e-06

def reference(residual, attn_parts, norm_gain, routes, route_weights, w_gate, w_gate_q):
    hidden = residual.astype(jnp.float32) + lax.optimization_barrier(jnp.sum(attn_parts.astype(jnp.float32), axis=0))
    mean_square = lax.optimization_barrier(jnp.mean(hidden * hidden, axis=1, keepdims=True))
    normed = (hidden * lax.rsqrt(mean_square + epsilon) * norm_gain.astype(jnp.float32)[None, :]).astype(jnp.bfloat16)
    flat_routes = routes.reshape(-1).astype(jnp.int32)
    route_total = TOKENS * TOPK
    most_rows = N_EXPERT * CAP

    def per_expert(expert_id):
        chosen = flat_routes == expert_id
        positions = jnp.nonzero(chosen, size=most_rows, fill_value=route_total)[0].astype(jnp.int32)
        valid = positions < route_total
        token_rows = jnp.minimum(positions // TOPK, TOKENS - 1).astype(jnp.int32)
        picked = jnp.where(valid[:, None], normed[token_rows], jnp.zeros((), jnp.bfloat16))
        full_out = jnp.dot(picked, w_gate[expert_id], preferred_element_type=jnp.float32)
        quant_out = jnp.dot(picked, w_gate_q[expert_id], preferred_element_type=jnp.float32)
        difference = full_out - quant_out
        route_err = lax.optimization_barrier(jnp.mean(difference * difference, axis=1))
        route_pow = lax.optimization_barrier(jnp.mean(full_out * full_out, axis=1))
        load_count = jnp.sum(chosen.astype(jnp.float32))
        picked_wide = picked.astype(jnp.float32)
        hess_row = 2.0 * lax.optimization_barrier(jnp.sum(picked_wide * picked_wide, axis=0)) / load_count
        return (positions, route_err, route_pow, hess_row)
    positions, route_err, route_pow, hess_diag = lax.map(per_expert, jnp.arange(EXPERTS, dtype=jnp.int32))
    expert_error = lax.optimization_barrier(jnp.sum(route_err, axis=1)) / (lax.optimization_barrier(jnp.sum(route_pow, axis=1)) + epsilon)
    flat_positions = positions.reshape(-1)
    err_all = jnp.zeros((route_total,), jnp.float32).at[flat_positions].set(route_err.reshape(-1), mode='drop')
    pow_all = jnp.zeros((route_total,), jnp.float32).at[flat_positions].set(route_pow.reshape(-1), mode='drop')
    ratios = (err_all / (pow_all + epsilon)).reshape(TOKENS, TOPK)
    token_error = lax.optimization_barrier(jnp.sum(route_weights * ratios, axis=1))
    return (token_error, expert_error, hess_diag)
```

```python
import jax
import jax.numpy as jnp
from jax import lax
from jax.sharding import PartitionSpec as P

D = 7168
FF = 2048
CAP = 24


epsilon = 1e-06


def per_device(residual, attn_parts, norm_gain, routes, route_weights, w_gate, w_gate_q):
    n_expert = lax.axis_size("expert")
    tok_count = residual.shape[0]
    local_cols = residual.shape[1]
    top_count = routes.shape[1]
    gain_local = norm_gain.astype(jnp.float32)[None, :]
    gain_full = lax.all_gather(norm_gain, "tensor", tiled=True).astype(jnp.float32)[None, :]
    summed = lax.psum_scatter(
        attn_parts[0].astype(jnp.float32).astype(jnp.bfloat16),
        "tensor",
        scatter_dimension=1,
        tiled=True,
    ).astype(jnp.float32)
    hidden = (residual.astype(jnp.float32) + summed).astype(jnp.bfloat16)
    expert_ids = jnp.arange(n_expert, dtype=jnp.int32)
    flat_routes = routes.reshape(-1)
    one_hot = (flat_routes[:, None] == expert_ids[None, :]).astype(jnp.int32)
    earlier = jnp.cumsum(one_hot, axis=0) - one_hot
    slot_index = jnp.sum(earlier * one_hot, axis=1)
    target = flat_routes * CAP + slot_index
    load_counts = jnp.sum(one_hot, axis=0)
    slot_ids = jnp.arange(n_expert * CAP, dtype=jnp.int32)
    placing = (slot_ids[:, None] == target[None, :]).reshape(n_expert * CAP, tok_count, top_count)
    dispatch = jnp.sum(placing.astype(jnp.int32), axis=2).astype(jnp.bfloat16)
    outgoing = jnp.dot(dispatch, hidden, preferred_element_type=jnp.float32).astype(jnp.bfloat16)
    outgoing = outgoing.reshape(n_expert, CAP, local_cols)
    count_rows = jnp.broadcast_to(load_counts.astype(jnp.bfloat16)[:, None, None], (n_expert, 1, local_cols))
    outgoing = jnp.concatenate([outgoing, count_rows], axis=1)
    arrived = lax.all_to_all(outgoing, "expert", split_axis=0, concat_axis=0, tiled=True)
    arrived_counts = arrived[:, CAP, 0].astype(jnp.float32)
    own_block = arrived[:, :CAP, :].reshape(n_expert * CAP, local_cols)
    column_block = lax.all_gather(own_block, "tensor", axis=1, tiled=True)
    wide = column_block.astype(jnp.float32)
    scaling = lax.rsqrt(jnp.sum(wide * wide, axis=1, keepdims=True) / D + epsilon)
    normed = (wide * scaling * gain_full).astype(jnp.bfloat16)
    normed_local = (own_block.astype(jnp.float32) * scaling * gain_local).astype(jnp.bfloat16)
    full_acc = jnp.dot(normed, w_gate[0], preferred_element_type=jnp.float32)
    quant_acc = jnp.dot(normed, w_gate_q[0], preferred_element_type=jnp.float32)
    block_squares = jnp.einsum("rc,rc->c", normed_local, normed_local, preferred_element_type=jnp.float32)
    total_load = jnp.sum(arrived_counts)
    hess_local = 2.0 * block_squares / total_load
    difference = full_acc - quant_acc
    err_part = (jnp.sum(difference * difference, axis=1) / FF).reshape(n_expert, 1, CAP)
    pow_part = (jnp.sum(full_acc * full_acc, axis=1) / FF).reshape(n_expert, 1, CAP)
    slots = lax.psum(jnp.concatenate([err_part, pow_part], axis=1), "tensor")
    expert_total = jnp.sum(slots[:, 0]) / (jnp.sum(slots[:, 1]) + epsilon)
    back = lax.all_to_all(slots, "expert", split_axis=0, concat_axis=0, tiled=True)
    token_err = jnp.take(back[:, 0].reshape(-1), target).reshape(tok_count, top_count)
    token_pow = jnp.take(back[:, 1].reshape(-1), target).reshape(tok_count, top_count)
    ratios = token_err / (token_pow + epsilon)
    token_error = jnp.sum(route_weights * ratios, axis=1)
    return (token_error, expert_total.reshape(1), hess_local.reshape(1, local_cols))


def solution(mesh):
    placed = (
        P("expert", "tensor"),
        P("tensor", "expert", None),
        P("tensor"),
        P("expert", None),
        P("expert", None),
        P("expert", None, "tensor"),
        P("expert", None, "tensor"),
    )
    return jax.shard_map(
        per_device,
        mesh=mesh,
        in_specs=placed,
        out_specs=(P("expert"), P("expert"), P("expert", "tensor")),
        check_vma=False,
    )
```

```python
import jax
import jax.numpy as jnp
from jax import lax
from jax.experimental import pallas as pl
from jax.experimental.pallas import tpu as pltpu
from jax.sharding import PartitionSpec as P

D = 7168
FF = 2048
CAP = 24


epsilon = 1e-06

MESH_ID = pl.DeviceIdType.MESH


def exchange(x, axis, n, cid, gather):
    block = x.shape if gather else x.shape[1:]

    def kernel(x_ref, o_ref, local_sem, send_sem, recv_sem):
        me = lax.axis_index(axis)
        barrier = pltpu.get_barrier_semaphore()
        for k in range(1, n):
            pl.semaphore_signal(barrier, inc=1, device_id={axis: lax.rem(me + k, n)}, device_id_type=MESH_ID)
        pl.semaphore_wait(barrier, n - 1)
        local = pltpu.make_async_copy(x_ref if gather else x_ref.at[me], o_ref.at[me], local_sem)
        local.start()
        copies = []
        for k in range(1, n):
            peer = lax.rem(me + k, n)
            copy = pltpu.make_async_remote_copy(
                src_ref=x_ref if gather else x_ref.at[peer],
                dst_ref=o_ref.at[me],
                send_sem=send_sem.at[k],
                recv_sem=recv_sem.at[k],
                device_id={axis: peer},
                device_id_type=MESH_ID,
            )
            copy.start()
            copies.append(copy)
        local.wait()
        for copy in copies:
            copy.wait()

    return pl.pallas_call(
        kernel,
        out_shape=jax.ShapeDtypeStruct((n,) + tuple(block), x.dtype),
        in_specs=[pl.BlockSpec(memory_space=pltpu.VMEM)],
        out_specs=pl.BlockSpec(memory_space=pltpu.VMEM),
        scratch_shapes=[
            pltpu.SemaphoreType.DMA(()),
            pltpu.SemaphoreType.DMA((n,)),
            pltpu.SemaphoreType.DMA((n,)),
        ],
        compiler_params=pltpu.CompilerParams(collective_id=cid, has_side_effects=True),
    )(x)


def per_device(residual, attn_parts, norm_gain, routes, route_weights, w_gate, w_gate_q):
    n_expert = lax.axis_size("expert")
    n_tensor = lax.axis_size("tensor")
    tok_count = residual.shape[0]
    local_cols = residual.shape[1]
    top_count = routes.shape[1]
    gain_local = norm_gain.astype(jnp.float32)[None, :]
    gain_full = lax.all_gather(norm_gain, "tensor", tiled=True).astype(jnp.float32)[None, :]
    summed = lax.psum_scatter(
        attn_parts[0].astype(jnp.float32).astype(jnp.bfloat16),
        "tensor",
        scatter_dimension=1,
        tiled=True,
    ).astype(jnp.float32)
    hidden = (residual.astype(jnp.float32) + summed).astype(jnp.bfloat16)
    expert_ids = jnp.arange(n_expert, dtype=jnp.int32)
    flat_routes = routes.reshape(-1)
    one_hot = (flat_routes[:, None] == expert_ids[None, :]).astype(jnp.int32)
    earlier = jnp.cumsum(one_hot, axis=0) - one_hot
    slot_index = jnp.sum(earlier * one_hot, axis=1)
    target = flat_routes * CAP + slot_index
    load_counts = jnp.sum(one_hot, axis=0)
    slot_ids = jnp.arange(n_expert * CAP, dtype=jnp.int32)
    placing = (slot_ids[:, None] == target[None, :]).reshape(n_expert * CAP, tok_count, top_count)
    dispatch = jnp.sum(placing.astype(jnp.int32), axis=2).astype(jnp.bfloat16)
    outgoing = jnp.dot(dispatch, hidden, preferred_element_type=jnp.float32).astype(jnp.bfloat16)
    outgoing = outgoing.reshape(n_expert, CAP, local_cols)
    count_rows = jnp.broadcast_to(load_counts.astype(jnp.bfloat16)[:, None, None], (n_expert, 1, local_cols))
    outgoing = jnp.concatenate([outgoing, count_rows], axis=1)
    arrived = lax.all_to_all(outgoing, "expert", split_axis=0, concat_axis=0, tiled=True)
    arrived_counts = arrived[:, CAP, 0].astype(jnp.float32)
    own_block = arrived[:, :CAP, :].reshape(n_expert * CAP, local_cols)
    column_block = lax.all_gather(own_block, "tensor", axis=1, tiled=True)
    wide = column_block.astype(jnp.float32)
    scaling = lax.rsqrt(jnp.sum(wide * wide, axis=1, keepdims=True) / D + epsilon)
    normed = (wide * scaling * gain_full).astype(jnp.bfloat16)
    normed_local = (own_block.astype(jnp.float32) * scaling * gain_local).astype(jnp.bfloat16)
    full_acc = jnp.dot(normed, w_gate[0], preferred_element_type=jnp.float32)
    quant_acc = jnp.dot(normed, w_gate_q[0], preferred_element_type=jnp.float32)
    block_squares = jnp.einsum("rc,rc->c", normed_local, normed_local, preferred_element_type=jnp.float32)
    total_load = jnp.sum(arrived_counts)
    hess_local = 2.0 * block_squares / total_load
    difference = full_acc - quant_acc
    err_part = (jnp.sum(difference * difference, axis=1) / FF).reshape(n_expert, 1, CAP)
    pow_part = (jnp.sum(full_acc * full_acc, axis=1) / FF).reshape(n_expert, 1, CAP)
    partial = jnp.concatenate([err_part, pow_part], axis=1)
    slots = jnp.sum(exchange(partial, "tensor", n_tensor, 0, True), axis=0)
    expert_total = jnp.sum(slots[:, 0]) / (jnp.sum(slots[:, 1]) + epsilon)
    back = exchange(slots, "expert", n_expert, 1, False)
    token_err = jnp.take(back[:, 0].reshape(-1), target).reshape(tok_count, top_count)
    token_pow = jnp.take(back[:, 1].reshape(-1), target).reshape(tok_count, top_count)
    ratios = token_err / (token_pow + epsilon)
    token_error = jnp.sum(route_weights * ratios, axis=1)
    return (token_error, expert_total.reshape(1), hess_local.reshape(1, local_cols))


def solution(mesh):
    placed = (
        P("expert", "tensor"),
        P("tensor", "expert", None),
        P("tensor"),
        P("expert", None),
        P("expert", None),
        P("expert", None, "tensor"),
        P("expert", None, "tensor"),
    )
    return jax.shard_map(
        per_device,
        mesh=mesh,
        in_specs=placed,
        out_specs=(P("expert"), P("expert"), P("expert", "tensor")),
        check_vma=False,
    )
```

```python
import jax
import jax.numpy as jnp
from jax import lax
from jax.experimental import pallas as pl
from jax.experimental.pallas import tpu as pltpu
from jax.sharding import PartitionSpec as P

D = 7168
FF = 2048
CAP = 24


epsilon = 1e-06

MESH_ID = pl.DeviceIdType.MESH


def exchange(arrays, axis, n, cid):
    count = len(arrays)
    modes = [gather for _, gather in arrays]

    def kernel(*refs):
        x_refs = refs[:count]
        o_refs = refs[count:2 * count]
        local_sem, send_sem, recv_sem = refs[2 * count:]
        me = lax.axis_index(axis)
        barrier = pltpu.get_barrier_semaphore()
        for k in range(1, n):
            pl.semaphore_signal(barrier, inc=1, device_id={axis: lax.rem(me + k, n)}, device_id_type=MESH_ID)
        pl.semaphore_wait(barrier, n - 1)
        copies = []
        for a in range(count):
            x_ref, o_ref, gather = x_refs[a], o_refs[a], modes[a]
            local = pltpu.make_async_copy(x_ref if gather else x_ref.at[me], o_ref.at[me], local_sem.at[a])
            local.start()
            copies.append(local)
        for k in range(1, n):
            peer = lax.rem(me + k, n)
            for a in range(count):
                x_ref, o_ref, gather = x_refs[a], o_refs[a], modes[a]
                copy = pltpu.make_async_remote_copy(
                    src_ref=x_ref if gather else x_ref.at[peer],
                    dst_ref=o_ref.at[me],
                    send_sem=send_sem.at[a, k],
                    recv_sem=recv_sem.at[a, k],
                    device_id={axis: peer},
                    device_id_type=MESH_ID,
                )
                copy.start()
                copies.append(copy)
        for copy in copies:
            copy.wait()

    out_shape = [
        jax.ShapeDtypeStruct((n,) + tuple(x.shape if gather else x.shape[1:]), x.dtype)
        for x, gather in arrays
    ]
    return pl.pallas_call(
        kernel,
        out_shape=out_shape,
        in_specs=[pl.BlockSpec(memory_space=pltpu.VMEM)] * count,
        out_specs=[pl.BlockSpec(memory_space=pltpu.VMEM)] * count,
        scratch_shapes=[
            pltpu.SemaphoreType.DMA((count,)),
            pltpu.SemaphoreType.DMA((count, n)),
            pltpu.SemaphoreType.DMA((count, n)),
        ],
        compiler_params=pltpu.CompilerParams(collective_id=cid, has_side_effects=True),
    )(*[x for x, _ in arrays])


def per_device(residual, attn_parts, norm_gain, routes, route_weights, w_gate, w_gate_q):
    n_expert = lax.axis_size("expert")
    n_tensor = lax.axis_size("tensor")
    tok_count = residual.shape[0]
    local_cols = residual.shape[1]
    top_count = routes.shape[1]
    gain_local = norm_gain.astype(jnp.float32)[None, :]
    column_parts = attn_parts[0].reshape(tok_count, n_tensor, local_cols).transpose(1, 0, 2)
    parts_in, gain_in = exchange([(column_parts, False), (norm_gain.reshape(1, local_cols), True)], "tensor", n_tensor, 0)
    gain_full = gain_in.reshape(1, n_tensor * local_cols).astype(jnp.float32)
    summed = jnp.sum(parts_in.astype(jnp.float32), axis=0)
    hidden = (residual.astype(jnp.float32) + summed).astype(jnp.bfloat16)
    expert_ids = jnp.arange(n_expert, dtype=jnp.int32)
    flat_routes = routes.reshape(-1)
    one_hot = (flat_routes[:, None] == expert_ids[None, :]).astype(jnp.int32)
    earlier = jnp.cumsum(one_hot, axis=0) - one_hot
    slot_index = jnp.sum(earlier * one_hot, axis=1)
    target = flat_routes * CAP + slot_index
    load_counts = jnp.sum(one_hot, axis=0)
    slot_ids = jnp.arange(n_expert * CAP, dtype=jnp.int32)
    placing = (slot_ids[:, None] == target[None, :]).reshape(n_expert * CAP, tok_count, top_count)
    dispatch = jnp.sum(placing.astype(jnp.int32), axis=2).astype(jnp.bfloat16)
    outgoing = jnp.dot(dispatch, hidden, preferred_element_type=jnp.float32).astype(jnp.bfloat16)
    outgoing = outgoing.reshape(n_expert, CAP, local_cols)
    count_rows = jnp.broadcast_to(load_counts.astype(jnp.bfloat16)[:, None, None], (n_expert, 1, local_cols))
    outgoing = jnp.concatenate([outgoing, count_rows], axis=1)
    (arrived,) = exchange([(outgoing, False)], "expert", n_expert, 1)
    arrived_counts = arrived[:, CAP, 0].astype(jnp.float32)
    own_block = arrived[:, :CAP, :].reshape(n_expert * CAP, local_cols)
    column_block = lax.all_gather(own_block, "tensor", axis=1, tiled=True)
    wide = column_block.astype(jnp.float32)
    scaling = lax.rsqrt(jnp.sum(wide * wide, axis=1, keepdims=True) / D + epsilon)
    normed = (wide * scaling * gain_full).astype(jnp.bfloat16)
    normed_local = (own_block.astype(jnp.float32) * scaling * gain_local).astype(jnp.bfloat16)
    full_acc = jnp.dot(normed, w_gate[0], preferred_element_type=jnp.float32)
    quant_acc = jnp.dot(normed, w_gate_q[0], preferred_element_type=jnp.float32)
    block_squares = jnp.einsum("rc,rc->c", normed_local, normed_local, preferred_element_type=jnp.float32)
    total_load = jnp.sum(arrived_counts)
    hess_local = 2.0 * block_squares / total_load
    difference = full_acc - quant_acc
    err_part = (jnp.sum(difference * difference, axis=1) / FF).reshape(n_expert, 1, CAP)
    pow_part = (jnp.sum(full_acc * full_acc, axis=1) / FF).reshape(n_expert, 1, CAP)
    partial = jnp.concatenate([err_part, pow_part], axis=1)
    (gathered,) = exchange([(partial, True)], "tensor", n_tensor, 2)
    slots = jnp.sum(gathered, axis=0)
    expert_total = jnp.sum(slots[:, 0]) / (jnp.sum(slots[:, 1]) + epsilon)
    (back,) = exchange([(slots, False)], "expert", n_expert, 3)
    token_err = jnp.take(back[:, 0].reshape(-1), target).reshape(tok_count, top_count)
    token_pow = jnp.take(back[:, 1].reshape(-1), target).reshape(tok_count, top_count)
    ratios = token_err / (token_pow + epsilon)
    token_error = jnp.sum(route_weights * ratios, axis=1)
    return (token_error, expert_total.reshape(1), hess_local.reshape(1, local_cols))


def solution(mesh):
    placed = (
        P("expert", "tensor"),
        P("tensor", "expert", None),
        P("tensor"),
        P("expert", None),
        P("expert", None),
        P("expert", None, "tensor"),
        P("expert", None, "tensor"),
    )
    return jax.shard_map(
        per_device,
        mesh=mesh,
        in_specs=placed,
        out_specs=(P("expert"), P("expert"), P("expert", "tensor")),
        check_vma=False,
    )
```

```python
import jax
import jax.numpy as jnp
from jax import lax
from jax.experimental import pallas as pl
from jax.experimental.pallas import tpu as pltpu
from jax.sharding import PartitionSpec as P

D = 7168
FF = 2048
CAP = 24


epsilon = 1e-06

MESH_ID = pl.DeviceIdType.MESH


def exchange(arrays, axis, n, cid):
    count = len(arrays)
    modes = [gather for _, gather in arrays]

    def kernel(*refs):
        x_refs = refs[:count]
        o_refs = refs[count:2 * count]
        local_sem, send_sem, recv_sem = refs[2 * count:]
        me = lax.axis_index(axis)
        barrier = pltpu.get_barrier_semaphore()
        for k in range(1, n):
            pl.semaphore_signal(barrier, inc=1, device_id={axis: lax.rem(me + k, n)}, device_id_type=MESH_ID)
        pl.semaphore_wait(barrier, n - 1)
        copies = []
        for a in range(count):
            x_ref, o_ref, gather = x_refs[a], o_refs[a], modes[a]
            local = pltpu.make_async_copy(x_ref if gather else x_ref.at[me], o_ref.at[me], local_sem.at[a])
            local.start()
            copies.append(local)
        for k in range(1, n):
            peer = lax.rem(me + k, n)
            for a in range(count):
                x_ref, o_ref, gather = x_refs[a], o_refs[a], modes[a]
                copy = pltpu.make_async_remote_copy(
                    src_ref=x_ref if gather else x_ref.at[peer],
                    dst_ref=o_ref.at[me],
                    send_sem=send_sem.at[a, k],
                    recv_sem=recv_sem.at[a, k],
                    device_id={axis: peer},
                    device_id_type=MESH_ID,
                )
                copy.start()
                copies.append(copy)
        for copy in copies:
            copy.wait()

    out_shape = [
        jax.ShapeDtypeStruct((n,) + tuple(x.shape if gather else x.shape[1:]), x.dtype)
        for x, gather in arrays
    ]
    return pl.pallas_call(
        kernel,
        out_shape=out_shape,
        in_specs=[pl.BlockSpec(memory_space=pltpu.VMEM)] * count,
        out_specs=[pl.BlockSpec(memory_space=pltpu.VMEM)] * count,
        scratch_shapes=[
            pltpu.SemaphoreType.DMA((count,)),
            pltpu.SemaphoreType.DMA((count, n)),
            pltpu.SemaphoreType.DMA((count, n)),
        ],
        compiler_params=pltpu.CompilerParams(collective_id=cid, has_side_effects=True),
    )(*[x for x, _ in arrays])


def per_device(residual, attn_parts, norm_gain, routes, route_weights, w_gate, w_gate_q):
    n_expert = lax.axis_size("expert")
    n_tensor = lax.axis_size("tensor")
    tok_count = residual.shape[0]
    local_cols = residual.shape[1]
    top_count = routes.shape[1]
    gain_local = norm_gain.astype(jnp.float32)[None, :]
    column_parts = attn_parts[0].reshape(tok_count, n_tensor, local_cols).transpose(1, 0, 2)
    parts_in, gain_in = exchange([(column_parts, False), (norm_gain.reshape(1, local_cols), True)], "tensor", n_tensor, 0)
    gain_full = gain_in.reshape(1, n_tensor * local_cols).astype(jnp.float32)
    summed = jnp.sum(parts_in.astype(jnp.float32), axis=0)
    hidden = (residual.astype(jnp.float32) + summed).astype(jnp.bfloat16)
    expert_ids = jnp.arange(n_expert, dtype=jnp.int32)
    flat_routes = routes.reshape(-1)
    one_hot = (flat_routes[:, None] == expert_ids[None, :]).astype(jnp.int32)
    earlier = jnp.cumsum(one_hot, axis=0) - one_hot
    slot_index = jnp.sum(earlier * one_hot, axis=1)
    target = flat_routes * CAP + slot_index
    load_counts = jnp.sum(one_hot, axis=0)
    slot_ids = jnp.arange(n_expert * CAP, dtype=jnp.int32)
    placing = (slot_ids[:, None] == target[None, :]).reshape(n_expert * CAP, tok_count, top_count)
    dispatch = jnp.sum(placing.astype(jnp.int32), axis=2).astype(jnp.bfloat16)
    outgoing = jnp.dot(dispatch, hidden, preferred_element_type=jnp.float32).astype(jnp.bfloat16)
    lane_rows = CAP * local_cols // 128
    outgoing = outgoing.reshape(n_expert, lane_rows, 128)
    count_rows = jnp.broadcast_to(load_counts.astype(jnp.bfloat16)[:, None, None], (n_expert, 1, 128))
    outgoing = jnp.concatenate([outgoing, count_rows], axis=1)
    (arrived,) = exchange([(outgoing, False)], "expert", n_expert, 1)
    arrived_counts = arrived[:, lane_rows, 0].astype(jnp.float32)
    own_block = arrived[:, :lane_rows, :].reshape(n_expert * CAP, local_cols)
    column_block = lax.all_gather(own_block, "tensor", axis=1, tiled=True)
    wide = column_block.astype(jnp.float32)
    scaling = lax.rsqrt(jnp.sum(wide * wide, axis=1, keepdims=True) / D + epsilon)
    normed = (wide * scaling * gain_full).astype(jnp.bfloat16)
    normed_local = (own_block.astype(jnp.float32) * scaling * gain_local).astype(jnp.bfloat16)
    full_acc = jnp.dot(normed, w_gate[0], preferred_element_type=jnp.float32)
    quant_acc = jnp.dot(normed, w_gate_q[0], preferred_element_type=jnp.float32)
    block_squares = jnp.einsum("rc,rc->c", normed_local, normed_local, preferred_element_type=jnp.float32)
    total_load = jnp.sum(arrived_counts)
    hess_local = 2.0 * block_squares / total_load
    difference = full_acc - quant_acc
    err_part = jnp.sum(difference * difference, axis=1) / FF
    pow_part = jnp.sum(full_acc * full_acc, axis=1) / FF
    partial = jnp.concatenate([err_part, pow_part]).reshape(-1, 128)
    (gathered,) = exchange([(partial, True)], "tensor", n_tensor, 2)
    slots = jnp.sum(gathered, axis=0).reshape(2, n_expert, CAP).transpose(1, 0, 2)
    expert_total = jnp.sum(slots[:, 0]) / (jnp.sum(slots[:, 1]) + epsilon)
    (back,) = exchange([(slots, False)], "expert", n_expert, 3)
    token_err = jnp.take(back[:, 0].reshape(-1), target).reshape(tok_count, top_count)
    token_pow = jnp.take(back[:, 1].reshape(-1), target).reshape(tok_count, top_count)
    ratios = token_err / (token_pow + epsilon)
    token_error = jnp.sum(route_weights * ratios, axis=1)
    return (token_error, expert_total.reshape(1), hess_local.reshape(1, local_cols))


def solution(mesh):
    placed = (
        P("expert", "tensor"),
        P("tensor", "expert", None),
        P("tensor"),
        P("expert", None),
        P("expert", None),
        P("expert", None, "tensor"),
        P("expert", None, "tensor"),
    )
    return jax.shard_map(
        per_device,
        mesh=mesh,
        in_specs=placed,
        out_specs=(P("expert"), P("expert"), P("expert", "tensor")),
        check_vma=False,
    )
```

```python
import jax
import jax.numpy as jnp
from jax import lax
from jax.experimental import pallas as pl
from jax.experimental.pallas import tpu as pltpu
from jax.sharding import PartitionSpec as P

D = 7168
FF = 2048
CAP = 24


epsilon = 1e-06

MESH_ID = pl.DeviceIdType.MESH


def exchange(arrays, axis, n, cid):
    count = len(arrays)
    modes = [gather for _, gather in arrays]

    def kernel(*refs):
        x_refs = refs[:count]
        o_refs = refs[count:2 * count]
        local_sem, send_sem, recv_sem = refs[2 * count:]
        me = lax.axis_index(axis)
        barrier = pltpu.get_barrier_semaphore()
        for k in range(1, n):
            pl.semaphore_signal(barrier, inc=1, device_id={axis: lax.rem(me + k, n)}, device_id_type=MESH_ID)
        pl.semaphore_wait(barrier, n - 1)
        copies = []
        for a in range(count):
            x_ref, o_ref, gather = x_refs[a], o_refs[a], modes[a]
            local = pltpu.make_async_copy(x_ref if gather else x_ref.at[me], o_ref.at[me], local_sem.at[a])
            local.start()
            copies.append(local)
        for k in range(1, n):
            peer = lax.rem(me + k, n)
            for a in range(count):
                x_ref, o_ref, gather = x_refs[a], o_refs[a], modes[a]
                copy = pltpu.make_async_remote_copy(
                    src_ref=x_ref if gather else x_ref.at[peer],
                    dst_ref=o_ref.at[me],
                    send_sem=send_sem.at[a, k],
                    recv_sem=recv_sem.at[a, k],
                    device_id={axis: peer},
                    device_id_type=MESH_ID,
                )
                copy.start()
                copies.append(copy)
        for copy in copies:
            copy.wait()

    out_shape = [
        jax.ShapeDtypeStruct((n,) + tuple(x.shape if gather else x.shape[1:]), x.dtype)
        for x, gather in arrays
    ]
    return pl.pallas_call(
        kernel,
        out_shape=out_shape,
        in_specs=[pl.BlockSpec(memory_space=pltpu.VMEM)] * count,
        out_specs=[pl.BlockSpec(memory_space=pltpu.VMEM)] * count,
        scratch_shapes=[
            pltpu.SemaphoreType.DMA((count,)),
            pltpu.SemaphoreType.DMA((count, n)),
            pltpu.SemaphoreType.DMA((count, n)),
        ],
        compiler_params=pltpu.CompilerParams(collective_id=cid, has_side_effects=True),
    )(*[x for x, _ in arrays])


def per_device(residual, attn_parts, norm_gain, routes, route_weights, w_gate, w_gate_q):
    n_expert = lax.axis_size("expert")
    n_tensor = lax.axis_size("tensor")
    tok_count = residual.shape[0]
    local_cols = residual.shape[1]
    top_count = routes.shape[1]
    gain_local = norm_gain.astype(jnp.float32)[None, :]
    column_parts = attn_parts[0].reshape(tok_count, n_tensor, local_cols).transpose(1, 0, 2)
    parts_in, gain_in = exchange([(column_parts, False), (norm_gain.reshape(1, local_cols), True)], "tensor", n_tensor, 0)
    gain_full = gain_in.reshape(1, n_tensor * local_cols).astype(jnp.float32)
    summed = jnp.sum(parts_in.astype(jnp.float32), axis=0)
    hidden = (residual.astype(jnp.float32) + summed).astype(jnp.bfloat16)
    expert_ids = jnp.arange(n_expert, dtype=jnp.int32)
    flat_routes = routes.reshape(-1)
    one_hot = (flat_routes[:, None] == expert_ids[None, :]).astype(jnp.int32)
    earlier = jnp.cumsum(one_hot, axis=0) - one_hot
    slot_index = jnp.sum(earlier * one_hot, axis=1)
    target = flat_routes * CAP + slot_index
    load_counts = jnp.sum(one_hot, axis=0)
    slot_ids = jnp.arange(n_expert * CAP, dtype=jnp.int32)
    placing = (slot_ids[:, None] == target[None, :]).reshape(n_expert * CAP, tok_count, top_count)
    dispatch = jnp.sum(placing.astype(jnp.int32), axis=2).astype(jnp.bfloat16)
    outgoing = jnp.dot(dispatch, hidden, preferred_element_type=jnp.float32).astype(jnp.bfloat16)
    lane_rows = CAP * local_cols // 128
    outgoing = outgoing.reshape(n_expert, lane_rows, 128)
    count_rows = jnp.broadcast_to(load_counts.astype(jnp.bfloat16)[:, None, None], (n_expert, 1, 128))
    outgoing = jnp.concatenate([outgoing, count_rows], axis=1)
    (arrived,) = exchange([(outgoing, False)], "expert", n_expert, 1)
    arrived_counts = arrived[:, lane_rows, 0].astype(jnp.float32)
    own_block = arrived[:, :lane_rows, :].reshape(n_expert * CAP, local_cols)
    halves = 2
    half_rows = n_expert * CAP // halves
    err_parts, pow_parts, square_parts = [], [], []
    gathered_rows = [
        lax.all_gather(own_block[h * half_rows:(h + 1) * half_rows], "tensor", axis=1, tiled=True)
        for h in range(halves)
    ]
    for h in range(halves):
        rows = own_block[h * half_rows:(h + 1) * half_rows]
        column_block = gathered_rows[h]
        if h > 0:
            column_block, err_parts[-1], pow_parts[-1], square_parts[-1] = lax.optimization_barrier(
                (column_block, err_parts[-1], pow_parts[-1], square_parts[-1])
            )
        wide = column_block.astype(jnp.float32)
        scaling = lax.rsqrt(jnp.sum(wide * wide, axis=1, keepdims=True) / D + epsilon)
        normed = (wide * scaling * gain_full).astype(jnp.bfloat16)
        normed_local = (rows.astype(jnp.float32) * scaling * gain_local).astype(jnp.bfloat16)
        full_acc = jnp.dot(normed, w_gate[0], preferred_element_type=jnp.float32)
        quant_acc = jnp.dot(normed, w_gate_q[0], preferred_element_type=jnp.float32)
        square_parts.append(jnp.einsum("rc,rc->c", normed_local, normed_local, preferred_element_type=jnp.float32))
        difference = full_acc - quant_acc
        err_parts.append(jnp.sum(difference * difference, axis=1) / FF)
        pow_parts.append(jnp.sum(full_acc * full_acc, axis=1) / FF)
    block_squares = square_parts[0]
    for h in range(1, halves):
        block_squares = block_squares + square_parts[h]
    total_load = jnp.sum(arrived_counts)
    hess_local = 2.0 * block_squares / total_load
    err_part = jnp.concatenate(err_parts)
    pow_part = jnp.concatenate(pow_parts)
    partial = jnp.concatenate([err_part, pow_part]).reshape(-1, 128)
    (gathered,) = exchange([(partial, True)], "tensor", n_tensor, 2)
    slots = jnp.sum(gathered, axis=0).reshape(2, n_expert, CAP).transpose(1, 0, 2)
    expert_total = jnp.sum(slots[:, 0]) / (jnp.sum(slots[:, 1]) + epsilon)
    (back,) = exchange([(slots, False)], "expert", n_expert, 3)
    token_err = jnp.take(back[:, 0].reshape(-1), target).reshape(tok_count, top_count)
    token_pow = jnp.take(back[:, 1].reshape(-1), target).reshape(tok_count, top_count)
    ratios = token_err / (token_pow + epsilon)
    token_error = jnp.sum(route_weights * ratios, axis=1)
    return (token_error, expert_total.reshape(1), hess_local.reshape(1, local_cols))


def solution(mesh):
    placed = (
        P("expert", "tensor"),
        P("tensor", "expert", None),
        P("tensor"),
        P("expert", None),
        P("expert", None),
        P("expert", None, "tensor"),
        P("expert", None, "tensor"),
    )
    return jax.shard_map(
        per_device,
        mesh=mesh,
        in_specs=placed,
        out_specs=(P("expert"), P("expert"), P("expert", "tensor")),
        check_vma=False,
    )
```

```python
import jax
import jax.numpy as jnp
from jax import lax
from jax.experimental import pallas as pl
from jax.experimental.pallas import tpu as pltpu
from jax.sharding import PartitionSpec as P

D = 7168
FF = 2048
CAP = 24


epsilon = 1e-06

MESH_ID = pl.DeviceIdType.MESH


def exchange(arrays, axis, cid, size, stride=1):
    count = len(arrays)
    modes = [gather for _, gather in arrays]

    def kernel(*refs):
        x_refs = refs[:count]
        o_refs = refs[count:2 * count]
        local_sem, send_sem, recv_sem = refs[2 * count:]
        me = lax.axis_index(axis)
        pos = lax.rem(lax.div(me, stride), size)
        base = me - pos * stride

        def member(k):
            return base + lax.rem(pos + k, size) * stride

        barrier = pltpu.get_barrier_semaphore()
        for k in range(1, size):
            pl.semaphore_signal(barrier, inc=1, device_id={axis: member(k)}, device_id_type=MESH_ID)
        pl.semaphore_wait(barrier, size - 1)
        copies = []
        for a in range(count):
            x_ref, o_ref, gather = x_refs[a], o_refs[a], modes[a]
            local = pltpu.make_async_copy(x_ref if gather else x_ref.at[pos], o_ref.at[pos], local_sem.at[a])
            local.start()
            copies.append(local)
        for k in range(1, size):
            peer_pos = lax.rem(pos + k, size)
            for a in range(count):
                x_ref, o_ref, gather = x_refs[a], o_refs[a], modes[a]
                copy = pltpu.make_async_remote_copy(
                    src_ref=x_ref if gather else x_ref.at[peer_pos],
                    dst_ref=o_ref.at[pos],
                    send_sem=send_sem.at[a, k],
                    recv_sem=recv_sem.at[a, k],
                    device_id={axis: member(k)},
                    device_id_type=MESH_ID,
                )
                copy.start()
                copies.append(copy)
        for copy in copies:
            copy.wait()

    out_shape = [
        jax.ShapeDtypeStruct((size,) + tuple(x.shape if gather else x.shape[1:]), x.dtype)
        for x, gather in arrays
    ]
    return pl.pallas_call(
        kernel,
        out_shape=out_shape,
        in_specs=[pl.BlockSpec(memory_space=pltpu.VMEM)] * count,
        out_specs=[pl.BlockSpec(memory_space=pltpu.VMEM)] * count,
        scratch_shapes=[
            pltpu.SemaphoreType.DMA((count,)),
            pltpu.SemaphoreType.DMA((count, size)),
            pltpu.SemaphoreType.DMA((count, size)),
        ],
        compiler_params=pltpu.CompilerParams(collective_id=cid, has_side_effects=True),
    )(*[x for x, _ in arrays])


def per_device(residual, attn_parts, norm_gain, routes, route_weights, w_gate, w_gate_q):
    n_expert = lax.axis_size("expert")
    n_tensor = lax.axis_size("tensor")
    tok_count = residual.shape[0]
    local_cols = residual.shape[1]
    top_count = routes.shape[1]
    gain_local = norm_gain.astype(jnp.float32)[None, :]
    n_chip = n_tensor // 2
    column_parts = attn_parts[0].reshape(tok_count, n_chip, 2, local_cols).transpose(2, 1, 0, 3)
    pair_in, gain_pair = exchange([(column_parts, False), (norm_gain.reshape(1, local_cols), True)], "tensor", 0, 2)
    pair_sum = (pair_in[0].astype(jnp.float32) + pair_in[1].astype(jnp.float32)).astype(jnp.bfloat16)
    parts_in, gain_in = exchange([(pair_sum, False), (gain_pair, True)], "tensor", 4, n_chip, 2)
    gain_full = gain_in.reshape(1, n_tensor * local_cols).astype(jnp.float32)
    summed = jnp.sum(parts_in.astype(jnp.float32), axis=0)
    hidden = (residual.astype(jnp.float32) + summed).astype(jnp.bfloat16)
    expert_ids = jnp.arange(n_expert, dtype=jnp.int32)
    flat_routes = routes.reshape(-1)
    one_hot = (flat_routes[:, None] == expert_ids[None, :]).astype(jnp.int32)
    earlier = jnp.cumsum(one_hot, axis=0) - one_hot
    slot_index = jnp.sum(earlier * one_hot, axis=1)
    target = flat_routes * CAP + slot_index
    load_counts = jnp.sum(one_hot, axis=0)
    slot_ids = jnp.arange(n_expert * CAP, dtype=jnp.int32)
    placing = (slot_ids[:, None] == target[None, :]).reshape(n_expert * CAP, tok_count, top_count)
    dispatch = jnp.sum(placing.astype(jnp.int32), axis=2).astype(jnp.bfloat16)
    outgoing = jnp.dot(dispatch, hidden, preferred_element_type=jnp.float32).astype(jnp.bfloat16)
    lane_rows = CAP * local_cols // 128
    outgoing = outgoing.reshape(n_expert, lane_rows, 128)
    count_rows = jnp.broadcast_to(load_counts.astype(jnp.bfloat16)[:, None, None], (n_expert, 1, 128))
    outgoing = jnp.concatenate([outgoing, count_rows], axis=1)
    (arrived,) = exchange([(outgoing, False)], "expert", 1, n_expert)
    arrived_counts = arrived[:, lane_rows, 0].astype(jnp.float32)
    own_block = arrived[:, :lane_rows, :].reshape(n_expert * CAP, local_cols)
    column_block = lax.all_gather(own_block, "tensor", axis=1, tiled=True)
    wide = column_block.astype(jnp.float32)
    scaling = lax.rsqrt(jnp.sum(wide * wide, axis=1, keepdims=True) / D + epsilon)
    normed = (wide * scaling * gain_full).astype(jnp.bfloat16)
    normed_local = (own_block.astype(jnp.float32) * scaling * gain_local).astype(jnp.bfloat16)
    full_acc = jnp.dot(normed, w_gate[0], preferred_element_type=jnp.float32)
    quant_acc = jnp.dot(normed, w_gate_q[0], preferred_element_type=jnp.float32)
    block_squares = jnp.einsum("rc,rc->c", normed_local, normed_local, preferred_element_type=jnp.float32)
    total_load = jnp.sum(arrived_counts)
    hess_local = 2.0 * block_squares / total_load
    difference = full_acc - quant_acc
    err_part = jnp.sum(difference * difference, axis=1) / FF
    pow_part = jnp.sum(full_acc * full_acc, axis=1) / FF
    partial = jnp.concatenate([err_part, pow_part]).reshape(-1, 128)
    (gathered,) = exchange([(partial, True)], "tensor", 2, n_tensor)
    slots = jnp.sum(gathered, axis=0).reshape(2, n_expert, CAP).transpose(1, 0, 2)
    expert_total = jnp.sum(slots[:, 0]) / (jnp.sum(slots[:, 1]) + epsilon)
    (back,) = exchange([(slots, False)], "expert", 3, n_expert)
    token_err = jnp.take(back[:, 0].reshape(-1), target).reshape(tok_count, top_count)
    token_pow = jnp.take(back[:, 1].reshape(-1), target).reshape(tok_count, top_count)
    ratios = token_err / (token_pow + epsilon)
    token_error = jnp.sum(route_weights * ratios, axis=1)
    return (token_error, expert_total.reshape(1), hess_local.reshape(1, local_cols))


def solution(mesh):
    placed = (
        P("expert", "tensor"),
        P("tensor", "expert", None),
        P("tensor"),
        P("expert", None),
        P("expert", None),
        P("expert", None, "tensor"),
        P("expert", None, "tensor"),
    )
    return jax.shard_map(
        per_device,
        mesh=mesh,
        in_specs=placed,
        out_specs=(P("expert"), P("expert"), P("expert", "tensor")),
        check_vma=False,
    )
```

```python
import jax
import jax.numpy as jnp
from jax import lax
from jax.experimental import pallas as pl
from jax.experimental.pallas import tpu as pltpu
from jax.sharding import PartitionSpec as P

D = 7168
FF = 2048
CAP = 24


epsilon = 1e-06

MESH_ID = pl.DeviceIdType.MESH


def exchange(arrays, axis, cid, size, stride=1):
    count = len(arrays)
    modes = [gather for _, gather in arrays]

    def kernel(*refs):
        x_refs = refs[:count]
        o_refs = refs[count:2 * count]
        local_sem, send_sem, recv_sem = refs[2 * count:]
        me = lax.axis_index(axis)
        pos = lax.rem(lax.div(me, stride), size)
        base = me - pos * stride

        def member(k):
            return base + lax.rem(pos + k, size) * stride

        barrier = pltpu.get_barrier_semaphore()
        for k in range(1, size):
            pl.semaphore_signal(barrier, inc=1, device_id={axis: member(k)}, device_id_type=MESH_ID)
        pl.semaphore_wait(barrier, size - 1)
        copies = []
        for a in range(count):
            x_ref, o_ref, gather = x_refs[a], o_refs[a], modes[a]
            local = pltpu.make_async_copy(x_ref if gather else x_ref.at[pos], o_ref.at[pos], local_sem.at[a])
            local.start()
            copies.append(local)
        for k in range(1, size):
            peer_pos = lax.rem(pos + k, size)
            for a in range(count):
                x_ref, o_ref, gather = x_refs[a], o_refs[a], modes[a]
                copy = pltpu.make_async_remote_copy(
                    src_ref=x_ref if gather else x_ref.at[peer_pos],
                    dst_ref=o_ref.at[pos],
                    send_sem=send_sem.at[a, k],
                    recv_sem=recv_sem.at[a, k],
                    device_id={axis: member(k)},
                    device_id_type=MESH_ID,
                )
                copy.start()
                copies.append(copy)
        for copy in copies:
            copy.wait()

    out_shape = [
        jax.ShapeDtypeStruct((size,) + tuple(x.shape if gather else x.shape[1:]), x.dtype)
        for x, gather in arrays
    ]
    return pl.pallas_call(
        kernel,
        out_shape=out_shape,
        in_specs=[pl.BlockSpec(memory_space=pltpu.VMEM)] * count,
        out_specs=[pl.BlockSpec(memory_space=pltpu.VMEM)] * count,
        scratch_shapes=[
            pltpu.SemaphoreType.DMA((count,)),
            pltpu.SemaphoreType.DMA((count, size)),
            pltpu.SemaphoreType.DMA((count, size)),
        ],
        compiler_params=pltpu.CompilerParams(collective_id=cid, has_side_effects=True),
    )(*[x for x, _ in arrays])


def per_device(residual, attn_parts, norm_gain, routes, route_weights, w_gate, w_gate_q):
    n_expert = lax.axis_size("expert")
    n_tensor = lax.axis_size("tensor")
    tok_count = residual.shape[0]
    local_cols = residual.shape[1]
    top_count = routes.shape[1]
    gain_local = norm_gain.astype(jnp.float32)[None, :]
    n_chip = n_tensor // 2
    column_parts = attn_parts[0].reshape(tok_count, n_chip, 2, local_cols).transpose(2, 1, 0, 3)
    pair_in, gain_pair = exchange([(column_parts, False), (norm_gain.reshape(1, local_cols), True)], "tensor", 0, 2)
    pair_sum = (pair_in[0].astype(jnp.float32) + pair_in[1].astype(jnp.float32)).astype(jnp.bfloat16)
    parts_in, gain_in = exchange([(pair_sum, False), (gain_pair, True)], "tensor", 4, n_chip, 2)
    gain_full = gain_in.reshape(1, n_tensor * local_cols).astype(jnp.float32)
    summed = jnp.sum(parts_in.astype(jnp.float32), axis=0)
    hidden = (residual.astype(jnp.float32) + summed).astype(jnp.bfloat16)
    expert_ids = jnp.arange(n_expert, dtype=jnp.int32)
    flat_routes = routes.reshape(-1)
    one_hot = (flat_routes[:, None] == expert_ids[None, :]).astype(jnp.int32)
    earlier = jnp.cumsum(one_hot, axis=0) - one_hot
    slot_index = jnp.sum(earlier * one_hot, axis=1)
    target = flat_routes * CAP + slot_index
    load_counts = jnp.sum(one_hot, axis=0)
    slot_ids = jnp.arange(n_expert * CAP, dtype=jnp.int32)
    placing = (slot_ids[:, None] == target[None, :]).reshape(n_expert * CAP, tok_count, top_count)
    dispatch = jnp.sum(placing.astype(jnp.int32), axis=2).astype(jnp.bfloat16)
    outgoing = jnp.dot(dispatch, hidden, preferred_element_type=jnp.float32).astype(jnp.bfloat16)
    lane_rows = CAP * local_cols // 128
    outgoing = outgoing.reshape(n_expert, lane_rows, 128)
    count_rows = jnp.broadcast_to(load_counts.astype(jnp.bfloat16)[:, None, None], (n_expert, 1, 128))
    outgoing = jnp.concatenate([outgoing, count_rows], axis=1)
    (arrived,) = exchange([(outgoing, False)], "expert", 1, n_expert)
    arrived_counts = arrived[:, lane_rows, 0].astype(jnp.float32)
    own_block = arrived[:, :lane_rows, :].reshape(n_expert * CAP, local_cols)
    column_block = lax.all_gather(own_block, "tensor", axis=1, tiled=True)
    wide = column_block.astype(jnp.float32)
    scaling = lax.rsqrt(jnp.sum(wide * wide, axis=1, keepdims=True) / D + epsilon)
    normed = (wide * scaling * gain_full).astype(jnp.bfloat16)
    normed_local = (own_block.astype(jnp.float32) * scaling * gain_local).astype(jnp.bfloat16)
    full_acc = jnp.dot(normed, w_gate[0], preferred_element_type=jnp.float32)
    quant_acc = jnp.dot(normed, w_gate_q[0], preferred_element_type=jnp.float32)
    block_squares = jnp.einsum("rc,rc->c", normed_local, normed_local, preferred_element_type=jnp.float32)
    total_load = jnp.sum(arrived_counts)
    hess_local = 2.0 * block_squares / total_load
    difference = full_acc - quant_acc
    err_part = jnp.sum(difference * difference, axis=1) / FF
    pow_part = jnp.sum(full_acc * full_acc, axis=1) / FF
    partial = jnp.concatenate([err_part, pow_part]).reshape(-1, 128)
    (gathered,) = exchange([(partial, True)], "tensor", 2, n_tensor)
    slots = jnp.sum(gathered, axis=0).reshape(2, n_expert, CAP).transpose(1, 0, 2)
    expert_total = jnp.sum(slots[:, 0]) / (jnp.sum(slots[:, 1]) + epsilon)
    slot_ratios = (slots[:, 0] / (slots[:, 1] + epsilon)).reshape(n_expert, 1, CAP)
    (back,) = exchange([(slot_ratios, False)], "expert", 3, n_expert)
    ratios = jnp.take(back.reshape(-1), target).reshape(tok_count, top_count)
    token_error = jnp.sum(route_weights * ratios, axis=1)
    return (token_error, expert_total.reshape(1), hess_local.reshape(1, local_cols))


def solution(mesh):
    placed = (
        P("expert", "tensor"),
        P("tensor", "expert", None),
        P("tensor"),
        P("expert", None),
        P("expert", None),
        P("expert", None, "tensor"),
        P("expert", None, "tensor"),
    )
    return jax.shard_map(
        per_device,
        mesh=mesh,
        in_specs=placed,
        out_specs=(P("expert"), P("expert"), P("expert", "tensor")),
        check_vma=False,
    )
```

```python
import jax
import jax.numpy as jnp
from jax import lax
from jax.experimental import pallas as pl
from jax.experimental.pallas import tpu as pltpu
from jax.sharding import PartitionSpec as P

D = 7168
FF = 2048
CAP = 24


epsilon = 1e-06

MESH_ID = pl.DeviceIdType.MESH


def exchange(arrays, axis, cid, size, stride=1):
    count = len(arrays)
    modes = [gather for _, gather in arrays]

    def kernel(*refs):
        x_refs = refs[:count]
        o_refs = refs[count:2 * count]
        local_sem, send_sem, recv_sem = refs[2 * count:]
        me = lax.axis_index(axis)
        pos = lax.rem(lax.div(me, stride), size)
        base = me - pos * stride

        def member(k):
            return base + lax.rem(pos + k, size) * stride

        barrier = pltpu.get_barrier_semaphore()
        for k in range(1, size):
            pl.semaphore_signal(barrier, inc=1, device_id={axis: member(k)}, device_id_type=MESH_ID)
        pl.semaphore_wait(barrier, size - 1)
        copies = []
        for a in range(count):
            x_ref, o_ref, gather = x_refs[a], o_refs[a], modes[a]
            local = pltpu.make_async_copy(x_ref if gather else x_ref.at[pos], o_ref.at[pos], local_sem.at[a])
            local.start()
            copies.append(local)
        for k in range(1, size):
            peer_pos = lax.rem(pos + k, size)
            for a in range(count):
                x_ref, o_ref, gather = x_refs[a], o_refs[a], modes[a]
                copy = pltpu.make_async_remote_copy(
                    src_ref=x_ref if gather else x_ref.at[peer_pos],
                    dst_ref=o_ref.at[pos],
                    send_sem=send_sem.at[a, k],
                    recv_sem=recv_sem.at[a, k],
                    device_id={axis: member(k)},
                    device_id_type=MESH_ID,
                )
                copy.start()
                copies.append(copy)
        for copy in copies:
            copy.wait()

    out_shape = [
        jax.ShapeDtypeStruct((size,) + tuple(x.shape if gather else x.shape[1:]), x.dtype)
        for x, gather in arrays
    ]
    return pl.pallas_call(
        kernel,
        out_shape=out_shape,
        in_specs=[pl.BlockSpec(memory_space=pltpu.VMEM)] * count,
        out_specs=[pl.BlockSpec(memory_space=pltpu.VMEM)] * count,
        scratch_shapes=[
            pltpu.SemaphoreType.DMA((count,)),
            pltpu.SemaphoreType.DMA((count, size)),
            pltpu.SemaphoreType.DMA((count, size)),
        ],
        compiler_params=pltpu.CompilerParams(collective_id=cid, has_side_effects=True),
    )(*[x for x, _ in arrays])


def per_device(residual, attn_parts, norm_gain, routes, route_weights, w_gate, w_gate_q):
    n_expert = lax.axis_size("expert")
    n_tensor = lax.axis_size("tensor")
    tok_count = residual.shape[0]
    local_cols = residual.shape[1]
    top_count = routes.shape[1]
    gain_local = norm_gain.astype(jnp.float32)[None, :]
    n_chip = n_tensor // 2
    column_parts = attn_parts[0].reshape(tok_count, n_chip, 2, local_cols).transpose(2, 1, 0, 3)
    pair_in, gain_pair = exchange([(column_parts, False), (norm_gain.reshape(1, local_cols), True)], "tensor", 0, 2)
    pair_sum = (pair_in[0].astype(jnp.float32) + pair_in[1].astype(jnp.float32)).astype(jnp.bfloat16)
    parts_in, gain_in = exchange([(pair_sum, False), (gain_pair, True)], "tensor", 4, n_chip, 2)
    gain_full = gain_in.reshape(1, n_tensor * local_cols).astype(jnp.float32)
    summed = jnp.sum(parts_in.astype(jnp.float32), axis=0)
    hidden = (residual.astype(jnp.float32) + summed).astype(jnp.bfloat16)
    expert_ids = jnp.arange(n_expert, dtype=jnp.int32)
    flat_routes = routes.reshape(-1)
    one_hot = (flat_routes[:, None] == expert_ids[None, :]).astype(jnp.int32)
    earlier = jnp.cumsum(one_hot, axis=0) - one_hot
    slot_index = jnp.sum(earlier * one_hot, axis=1)
    target = flat_routes * CAP + slot_index
    load_counts = jnp.sum(one_hot, axis=0)
    slot_ids = jnp.arange(n_expert * CAP, dtype=jnp.int32)
    placing = (slot_ids[:, None] == target[None, :]).reshape(n_expert * CAP, tok_count, top_count)
    dispatch = jnp.sum(placing.astype(jnp.int32), axis=2).astype(jnp.bfloat16)
    outgoing = jnp.dot(dispatch, hidden, preferred_element_type=jnp.float32).astype(jnp.bfloat16)
    lane_rows = CAP * local_cols // 128
    outgoing = outgoing.reshape(n_expert, lane_rows, 128)
    count_rows = jnp.broadcast_to(load_counts.astype(jnp.bfloat16)[:, None, None], (n_expert, 1, 128))
    outgoing = jnp.concatenate([outgoing, count_rows], axis=1)
    (arrived,) = exchange([(outgoing, False)], "expert", 1, n_expert)
    arrived_counts = arrived[:, lane_rows, 0].astype(jnp.float32)
    own_block = arrived[:, :lane_rows, :].reshape(n_expert * CAP, local_cols)
    slot_count = n_expert * CAP
    own_wide = own_block.astype(jnp.float32)
    own_squares = jnp.sum(own_wide * own_wide, axis=1)
    squares_hi = own_squares.astype(jnp.bfloat16)
    squares_lo = (own_squares - squares_hi.astype(jnp.float32)).astype(jnp.bfloat16)
    extra_rows = 16
    packed = jnp.concatenate([squares_hi, squares_lo])
    packed = jnp.pad(packed, (0, extra_rows * local_cols - 2 * slot_count)).reshape(extra_rows, local_cols)
    payload = jnp.concatenate([own_block, packed], axis=0)
    gathered_block = lax.all_gather(payload, "tensor", axis=1, tiled=True)
    column_block = gathered_block[:slot_count]
    packed_all = gathered_block[slot_count:].reshape(extra_rows, n_tensor, local_cols).transpose(1, 0, 2)
    packed_all = packed_all.reshape(n_tensor, extra_rows * local_cols)[:, :2 * slot_count].astype(jnp.float32)
    row_squares = jnp.sum(packed_all[:, :slot_count] + packed_all[:, slot_count:], axis=0)
    scaling = lax.rsqrt(row_squares[:, None] / D + epsilon)
    normed = (column_block.astype(jnp.float32) * scaling * gain_full).astype(jnp.bfloat16)
    normed_local = (own_block.astype(jnp.float32) * scaling * gain_local).astype(jnp.bfloat16)
    full_acc = jnp.dot(normed, w_gate[0], preferred_element_type=jnp.float32)
    quant_acc = jnp.dot(normed, w_gate_q[0], preferred_element_type=jnp.float32)
    block_squares = jnp.einsum("rc,rc->c", normed_local, normed_local, preferred_element_type=jnp.float32)
    total_load = jnp.sum(arrived_counts)
    hess_local = 2.0 * block_squares / total_load
    difference = full_acc - quant_acc
    err_part = jnp.sum(difference * difference, axis=1) / FF
    pow_part = jnp.sum(full_acc * full_acc, axis=1) / FF
    partial = jnp.concatenate([err_part, pow_part]).reshape(-1, 128)
    (gathered,) = exchange([(partial, True)], "tensor", 2, n_tensor)
    slots = jnp.sum(gathered, axis=0).reshape(2, n_expert, CAP).transpose(1, 0, 2)
    expert_total = jnp.sum(slots[:, 0]) / (jnp.sum(slots[:, 1]) + epsilon)
    slot_ratios = (slots[:, 0] / (slots[:, 1] + epsilon)).reshape(n_expert, 1, CAP)
    (back,) = exchange([(slot_ratios, False)], "expert", 3, n_expert)
    ratios = jnp.take(back.reshape(-1), target).reshape(tok_count, top_count)
    token_error = jnp.sum(route_weights * ratios, axis=1)
    return (token_error, expert_total.reshape(1), hess_local.reshape(1, local_cols))


def solution(mesh):
    placed = (
        P("expert", "tensor"),
        P("tensor", "expert", None),
        P("tensor"),
        P("expert", None),
        P("expert", None),
        P("expert", None, "tensor"),
        P("expert", None, "tensor"),
    )
    return jax.shard_map(
        per_device,
        mesh=mesh,
        in_specs=placed,
        out_specs=(P("expert"), P("expert"), P("expert", "tensor")),
        check_vma=False,
    )
```

```python
import jax
import jax.numpy as jnp
from jax import lax
from jax.experimental import pallas as pl
from jax.experimental.pallas import tpu as pltpu
from jax.sharding import PartitionSpec as P

D = 7168
FF = 2048
CAP = 24


epsilon = 1e-06

MESH_ID = pl.DeviceIdType.MESH


def exchange(arrays, axis, cid, size, stride=1):
    count = len(arrays)
    modes = [gather for _, gather in arrays]

    def kernel(*refs):
        x_refs = refs[:count]
        o_refs = refs[count:2 * count]
        local_sem, send_sem, recv_sem = refs[2 * count:]
        me = lax.axis_index(axis)
        pos = lax.rem(lax.div(me, stride), size)
        base = me - pos * stride

        def member(k):
            return base + lax.rem(pos + k, size) * stride

        barrier = pltpu.get_barrier_semaphore()
        for k in range(1, size):
            pl.semaphore_signal(barrier, inc=1, device_id={axis: member(k)}, device_id_type=MESH_ID)
        pl.semaphore_wait(barrier, size - 1)
        copies = []
        for a in range(count):
            x_ref, o_ref, gather = x_refs[a], o_refs[a], modes[a]
            local = pltpu.make_async_copy(x_ref if gather else x_ref.at[pos], o_ref.at[pos], local_sem.at[a])
            local.start()
            copies.append(local)
        for k in range(1, size):
            peer_pos = lax.rem(pos + k, size)
            for a in range(count):
                x_ref, o_ref, gather = x_refs[a], o_refs[a], modes[a]
                copy = pltpu.make_async_remote_copy(
                    src_ref=x_ref if gather else x_ref.at[peer_pos],
                    dst_ref=o_ref.at[pos],
                    send_sem=send_sem.at[a, k],
                    recv_sem=recv_sem.at[a, k],
                    device_id={axis: member(k)},
                    device_id_type=MESH_ID,
                )
                copy.start()
                copies.append(copy)
        for copy in copies:
            copy.wait()

    out_shape = [
        jax.ShapeDtypeStruct((size,) + tuple(x.shape if gather else x.shape[1:]), x.dtype)
        for x, gather in arrays
    ]
    return pl.pallas_call(
        kernel,
        out_shape=out_shape,
        in_specs=[pl.BlockSpec(memory_space=pltpu.VMEM)] * count,
        out_specs=[pl.BlockSpec(memory_space=pltpu.VMEM)] * count,
        scratch_shapes=[
            pltpu.SemaphoreType.DMA((count,)),
            pltpu.SemaphoreType.DMA((count, size)),
            pltpu.SemaphoreType.DMA((count, size)),
        ],
        compiler_params=pltpu.CompilerParams(collective_id=cid, has_side_effects=True),
    )(*[x for x, _ in arrays])


def per_device(residual, attn_parts, norm_gain, routes, route_weights, w_gate, w_gate_q):
    n_expert = lax.axis_size("expert")
    n_tensor = lax.axis_size("tensor")
    tok_count = residual.shape[0]
    local_cols = residual.shape[1]
    top_count = routes.shape[1]
    gain_local = norm_gain.astype(jnp.float32)[None, :]
    n_chip = n_tensor // 2
    column_parts = attn_parts[0].reshape(tok_count, n_chip, 2, local_cols).transpose(2, 1, 0, 3)
    pair_in, gain_pair = exchange([(column_parts, False), (norm_gain.reshape(1, local_cols), True)], "tensor", 0, 2)
    pair_sum = (pair_in[0].astype(jnp.float32) + pair_in[1].astype(jnp.float32)).astype(jnp.bfloat16)
    parts_in, gain_in = exchange([(pair_sum, False), (gain_pair, True)], "tensor", 4, n_chip, 2)
    gain_full = gain_in.reshape(1, n_tensor * local_cols).astype(jnp.float32)
    summed = jnp.sum(parts_in.astype(jnp.float32), axis=0)
    hidden = (residual.astype(jnp.float32) + summed).astype(jnp.bfloat16)
    expert_ids = jnp.arange(n_expert, dtype=jnp.int32)
    flat_routes = routes.reshape(-1)
    one_hot = (flat_routes[:, None] == expert_ids[None, :]).astype(jnp.int32)
    earlier = jnp.cumsum(one_hot, axis=0) - one_hot
    slot_index = jnp.sum(earlier * one_hot, axis=1)
    target = flat_routes * CAP + slot_index
    load_counts = jnp.sum(one_hot, axis=0)
    slot_ids = jnp.arange(n_expert * CAP, dtype=jnp.int32)
    placing = (slot_ids[:, None] == target[None, :]).reshape(n_expert * CAP, tok_count, top_count)
    dispatch = jnp.sum(placing.astype(jnp.int32), axis=2).astype(jnp.bfloat16)
    outgoing = jnp.dot(dispatch, hidden, preferred_element_type=jnp.float32).astype(jnp.bfloat16)
    lane_rows = CAP * local_cols // 128
    outgoing = outgoing.reshape(n_expert, lane_rows, 128)
    count_rows = jnp.broadcast_to(load_counts.astype(jnp.bfloat16)[:, None, None], (n_expert, 1, 128))
    outgoing = jnp.concatenate([outgoing, count_rows], axis=1)
    (arrived,) = exchange([(outgoing, False)], "expert", 1, n_expert)
    arrived_counts = arrived[:, lane_rows, 0].astype(jnp.float32)
    own_block = arrived[:, :lane_rows, :].reshape(n_expert * CAP, local_cols)
    column_block = lax.all_gather(own_block, "tensor", axis=1, tiled=True)
    wide = column_block.astype(jnp.float32)
    scaling = lax.rsqrt(jnp.sum(wide * wide, axis=1, keepdims=True) / D + epsilon)
    normed = (wide * scaling * gain_full).astype(jnp.bfloat16)
    normed_local = (own_block.astype(jnp.float32) * scaling * gain_local).astype(jnp.bfloat16)
    weight_cols = w_gate.shape[2]
    both_weights = jnp.concatenate([w_gate[0], w_gate_q[0]], axis=1)
    both_acc = jnp.dot(normed, both_weights, preferred_element_type=jnp.float32)
    full_acc = both_acc[:, :weight_cols]
    quant_acc = both_acc[:, weight_cols:]
    block_squares = jnp.einsum("rc,rc->c", normed_local, normed_local, preferred_element_type=jnp.float32)
    total_load = jnp.sum(arrived_counts)
    hess_local = 2.0 * block_squares / total_load
    difference = full_acc - quant_acc
    err_part = jnp.sum(difference * difference, axis=1) / FF
    pow_part = jnp.sum(full_acc * full_acc, axis=1) / FF
    partial = jnp.concatenate([err_part, pow_part]).reshape(-1, 128)
    (gathered,) = exchange([(partial, True)], "tensor", 2, n_tensor)
    slots = jnp.sum(gathered, axis=0).reshape(2, n_expert, CAP).transpose(1, 0, 2)
    expert_total = jnp.sum(slots[:, 0]) / (jnp.sum(slots[:, 1]) + epsilon)
    slot_ratios = (slots[:, 0] / (slots[:, 1] + epsilon)).reshape(n_expert, 1, CAP)
    (back,) = exchange([(slot_ratios, False)], "expert", 3, n_expert)
    ratios = jnp.take(back.reshape(-1), target).reshape(tok_count, top_count)
    token_error = jnp.sum(route_weights * ratios, axis=1)
    return (token_error, expert_total.reshape(1), hess_local.reshape(1, local_cols))


def solution(mesh):
    placed = (
        P("expert", "tensor"),
        P("tensor", "expert", None),
        P("tensor"),
        P("expert", None),
        P("expert", None),
        P("expert", None, "tensor"),
        P("expert", None, "tensor"),
    )
    return jax.shard_map(
        per_device,
        mesh=mesh,
        in_specs=placed,
        out_specs=(P("expert"), P("expert"), P("expert", "tensor")),
        check_vma=False,
    )
```

```python
import jax
import jax.numpy as jnp
from jax import lax
from jax.experimental import pallas as pl
from jax.experimental.pallas import tpu as pltpu
from jax.sharding import PartitionSpec as P

D = 7168
FF = 2048
CAP = 24


epsilon = 1e-06

MESH_ID = pl.DeviceIdType.MESH


def exchange(arrays, axis, cid, size, stride=1):
    count = len(arrays)
    modes = [gather for _, gather in arrays]

    def kernel(*refs):
        x_refs = refs[:count]
        o_refs = refs[count:2 * count]
        local_sem, send_sem, recv_sem = refs[2 * count:]
        me = lax.axis_index(axis)
        pos = lax.rem(lax.div(me, stride), size)
        base = me - pos * stride

        def member(k):
            return base + lax.rem(pos + k, size) * stride

        barrier = pltpu.get_barrier_semaphore()
        for k in range(1, size):
            pl.semaphore_signal(barrier, inc=1, device_id={axis: member(k)}, device_id_type=MESH_ID)
        pl.semaphore_wait(barrier, size - 1)
        copies = []
        for a in range(count):
            x_ref, o_ref, gather = x_refs[a], o_refs[a], modes[a]
            local = pltpu.make_async_copy(x_ref if gather else x_ref.at[pos], o_ref.at[pos], local_sem.at[a])
            local.start()
            copies.append(local)
        for k in range(1, size):
            peer_pos = lax.rem(pos + k, size)
            for a in range(count):
                x_ref, o_ref, gather = x_refs[a], o_refs[a], modes[a]
                copy = pltpu.make_async_remote_copy(
                    src_ref=x_ref if gather else x_ref.at[peer_pos],
                    dst_ref=o_ref.at[pos],
                    send_sem=send_sem.at[a, k],
                    recv_sem=recv_sem.at[a, k],
                    device_id={axis: member(k)},
                    device_id_type=MESH_ID,
                )
                copy.start()
                copies.append(copy)
        for copy in copies:
            copy.wait()

    out_shape = [
        jax.ShapeDtypeStruct((size,) + tuple(x.shape if gather else x.shape[1:]), x.dtype)
        for x, gather in arrays
    ]
    return pl.pallas_call(
        kernel,
        out_shape=out_shape,
        in_specs=[pl.BlockSpec(memory_space=pltpu.VMEM)] * count,
        out_specs=[pl.BlockSpec(memory_space=pltpu.VMEM)] * count,
        scratch_shapes=[
            pltpu.SemaphoreType.DMA((count,)),
            pltpu.SemaphoreType.DMA((count, size)),
            pltpu.SemaphoreType.DMA((count, size)),
        ],
        compiler_params=pltpu.CompilerParams(collective_id=cid, has_side_effects=True),
    )(*[x for x, _ in arrays])


def per_device(residual, attn_parts, norm_gain, routes, route_weights, w_gate, w_gate_q):
    n_expert = lax.axis_size("expert")
    n_tensor = lax.axis_size("tensor")
    tok_count = residual.shape[0]
    local_cols = residual.shape[1]
    top_count = routes.shape[1]
    gain_local = norm_gain.astype(jnp.float32)[None, :]
    n_chip = n_tensor // 2
    column_parts = attn_parts[0].reshape(tok_count, n_chip, 2, local_cols).transpose(2, 1, 0, 3)
    pair_in, gain_pair = exchange([(column_parts, False), (norm_gain.reshape(1, local_cols), True)], "tensor", 0, 2)
    pair_sum = (pair_in[0].astype(jnp.float32) + pair_in[1].astype(jnp.float32)).astype(jnp.bfloat16)
    parts_in, gain_in = exchange([(pair_sum, False), (gain_pair, True)], "tensor", 4, n_chip, 2)
    gain_full = gain_in.reshape(1, n_tensor * local_cols).astype(jnp.float32)
    summed = jnp.sum(parts_in.astype(jnp.float32), axis=0)
    hidden = (residual.astype(jnp.float32) + summed).astype(jnp.bfloat16)
    expert_ids = jnp.arange(n_expert, dtype=jnp.int32)
    flat_routes = routes.reshape(-1)
    one_hot = (flat_routes[:, None] == expert_ids[None, :]).astype(jnp.int32)
    earlier = jnp.cumsum(one_hot, axis=0) - one_hot
    slot_index = jnp.sum(earlier * one_hot, axis=1)
    target = flat_routes * CAP + slot_index
    load_counts = jnp.sum(one_hot, axis=0)
    slot_ids = jnp.arange(n_expert * CAP, dtype=jnp.int32)
    placing = (slot_ids[:, None] == target[None, :]).reshape(n_expert * CAP, tok_count, top_count)
    dispatch = jnp.sum(placing.astype(jnp.int32), axis=2).astype(jnp.bfloat16)
    outgoing = jnp.dot(dispatch, hidden, preferred_element_type=jnp.float32).astype(jnp.bfloat16)
    lane_rows = CAP * local_cols // 128
    outgoing = outgoing.reshape(n_expert, lane_rows, 128)
    count_rows = jnp.broadcast_to(load_counts.astype(jnp.bfloat16)[:, None, None], (n_expert, 1, 128))
    outgoing = jnp.concatenate([outgoing, count_rows], axis=1)
    (arrived,) = exchange([(outgoing, False)], "expert", 1, n_expert)
    arrived_counts = arrived[:, lane_rows, 0].astype(jnp.float32)
    own_block = arrived[:, :lane_rows, :].reshape(n_expert * CAP, local_cols)
    column_block = lax.all_gather(own_block, "tensor", axis=1, tiled=True)
    own_wide = own_block.astype(jnp.float32)
    own_squares = jnp.sum(own_wide * own_wide, axis=1).reshape(-1, 128)
    (squares_in,) = exchange([(own_squares, True)], "tensor", 6, n_tensor)
    row_squares = jnp.sum(squares_in, axis=0).reshape(-1, 1)
    scaling = lax.rsqrt(row_squares / D + epsilon)
    normed = (column_block.astype(jnp.float32) * scaling * gain_full).astype(jnp.bfloat16)
    normed_local = (own_block.astype(jnp.float32) * scaling * gain_local).astype(jnp.bfloat16)
    weight_cols = w_gate.shape[2]
    both_weights = jnp.concatenate([w_gate[0], w_gate_q[0]], axis=1)
    both_acc = jnp.dot(normed, both_weights, preferred_element_type=jnp.float32)
    full_acc = both_acc[:, :weight_cols]
    quant_acc = both_acc[:, weight_cols:]
    block_squares = jnp.einsum("rc,rc->c", normed_local, normed_local, preferred_element_type=jnp.float32)
    total_load = jnp.sum(arrived_counts)
    hess_local = 2.0 * block_squares / total_load
    difference = full_acc - quant_acc
    err_part = jnp.sum(difference * difference, axis=1) / FF
    pow_part = jnp.sum(full_acc * full_acc, axis=1) / FF
    partial = jnp.concatenate([err_part, pow_part]).reshape(-1, 128)
    (gathered,) = exchange([(partial, True)], "tensor", 2, n_tensor)
    slots = jnp.sum(gathered, axis=0).reshape(2, n_expert, CAP).transpose(1, 0, 2)
    expert_total = jnp.sum(slots[:, 0]) / (jnp.sum(slots[:, 1]) + epsilon)
    slot_ratios = (slots[:, 0] / (slots[:, 1] + epsilon)).reshape(n_expert, 1, CAP)
    (back,) = exchange([(slot_ratios, False)], "expert", 3, n_expert)
    ratios = jnp.take(back.reshape(-1), target).reshape(tok_count, top_count)
    token_error = jnp.sum(route_weights * ratios, axis=1)
    return (token_error, expert_total.reshape(1), hess_local.reshape(1, local_cols))


def solution(mesh):
    placed = (
        P("expert", "tensor"),
        P("tensor", "expert", None),
        P("tensor"),
        P("expert", None),
        P("expert", None),
        P("expert", None, "tensor"),
        P("expert", None, "tensor"),
    )
    return jax.shard_map(
        per_device,
        mesh=mesh,
        in_specs=placed,
        out_specs=(P("expert"), P("expert"), P("expert", "tensor")),
        check_vma=False,
    )
```

```python
import jax
import jax.numpy as jnp
from jax import lax
from jax.experimental import pallas as pl
from jax.experimental.pallas import tpu as pltpu
from jax.sharding import PartitionSpec as P

D = 7168
FF = 2048
CAP = 24


epsilon = 1e-06

MESH_ID = pl.DeviceIdType.MESH


def exchange(arrays, axis, cid, size, stride=1):
    count = len(arrays)
    modes = [gather for _, gather in arrays]

    def kernel(*refs):
        x_refs = refs[:count]
        o_refs = refs[count:2 * count]
        local_sem, send_sem, recv_sem = refs[2 * count:]
        me = lax.axis_index(axis)
        pos = lax.rem(lax.div(me, stride), size)
        base = me - pos * stride

        def member(k):
            return base + lax.rem(pos + k, size) * stride

        copies = []
        for a in range(count):
            x_ref, o_ref, gather = x_refs[a], o_refs[a], modes[a]
            local = pltpu.make_async_copy(x_ref if gather else x_ref.at[pos], o_ref.at[pos], local_sem.at[a])
            local.start()
            copies.append(local)
        for k in range(1, size):
            peer_pos = lax.rem(pos + k, size)
            for a in range(count):
                x_ref, o_ref, gather = x_refs[a], o_refs[a], modes[a]
                copy = pltpu.make_async_remote_copy(
                    src_ref=x_ref if gather else x_ref.at[peer_pos],
                    dst_ref=o_ref.at[pos],
                    send_sem=send_sem.at[a, k],
                    recv_sem=recv_sem.at[a, k],
                    device_id={axis: member(k)},
                    device_id_type=MESH_ID,
                )
                copy.start()
                copies.append(copy)
        for copy in copies:
            copy.wait()

    out_shape = [
        jax.ShapeDtypeStruct((size,) + tuple(x.shape if gather else x.shape[1:]), x.dtype)
        for x, gather in arrays
    ]
    return pl.pallas_call(
        kernel,
        out_shape=out_shape,
        in_specs=[pl.BlockSpec(memory_space=pltpu.VMEM)] * count,
        out_specs=[pl.BlockSpec(memory_space=pltpu.VMEM)] * count,
        scratch_shapes=[
            pltpu.SemaphoreType.DMA((count,)),
            pltpu.SemaphoreType.DMA((count, size)),
            pltpu.SemaphoreType.DMA((count, size)),
        ],
        compiler_params=pltpu.CompilerParams(has_side_effects=True),
    )(*[x for x, _ in arrays])


def per_device(residual, attn_parts, norm_gain, routes, route_weights, w_gate, w_gate_q):
    n_expert = lax.axis_size("expert")
    n_tensor = lax.axis_size("tensor")
    tok_count = residual.shape[0]
    local_cols = residual.shape[1]
    top_count = routes.shape[1]
    gain_local = norm_gain.astype(jnp.float32)[None, :]
    n_chip = n_tensor // 2
    column_parts = attn_parts[0].reshape(tok_count, n_chip, 2, local_cols).transpose(2, 1, 0, 3)
    pair_in, gain_pair = exchange([(column_parts, False), (norm_gain.reshape(1, local_cols), True)], "tensor", 0, 2)
    pair_sum = (pair_in[0].astype(jnp.float32) + pair_in[1].astype(jnp.float32)).astype(jnp.bfloat16)
    parts_in, gain_in = exchange([(pair_sum, False), (gain_pair, True)], "tensor", 4, n_chip, 2)
    gain_full = gain_in.reshape(1, n_tensor * local_cols).astype(jnp.float32)
    summed = jnp.sum(parts_in.astype(jnp.float32), axis=0)
    hidden = (residual.astype(jnp.float32) + summed).astype(jnp.bfloat16)
    expert_ids = jnp.arange(n_expert, dtype=jnp.int32)
    flat_routes = routes.reshape(-1)
    one_hot = (flat_routes[:, None] == expert_ids[None, :]).astype(jnp.int32)
    earlier = jnp.cumsum(one_hot, axis=0) - one_hot
    slot_index = jnp.sum(earlier * one_hot, axis=1)
    target = flat_routes * CAP + slot_index
    load_counts = jnp.sum(one_hot, axis=0)
    slot_ids = jnp.arange(n_expert * CAP, dtype=jnp.int32)
    placing = (slot_ids[:, None] == target[None, :]).reshape(n_expert * CAP, tok_count, top_count)
    dispatch = jnp.sum(placing.astype(jnp.int32), axis=2).astype(jnp.bfloat16)
    outgoing = jnp.dot(dispatch, hidden, preferred_element_type=jnp.float32).astype(jnp.bfloat16)
    lane_rows = CAP * local_cols // 128
    outgoing = outgoing.reshape(n_expert, lane_rows, 128)
    count_rows = jnp.broadcast_to(load_counts.astype(jnp.bfloat16)[:, None, None], (n_expert, 1, 128))
    outgoing = jnp.concatenate([outgoing, count_rows], axis=1)
    (arrived,) = exchange([(outgoing, False)], "expert", 1, n_expert)
    arrived_counts = arrived[:, lane_rows, 0].astype(jnp.float32)
    own_block = arrived[:, :lane_rows, :].reshape(n_expert * CAP, local_cols)
    column_block = lax.all_gather(own_block, "tensor", axis=1, tiled=True)
    own_wide = own_block.astype(jnp.float32)
    own_squares = jnp.sum(own_wide * own_wide, axis=1).reshape(-1, 128)
    (squares_in,) = exchange([(own_squares, True)], "tensor", 6, n_tensor)
    row_squares = jnp.sum(squares_in, axis=0).reshape(-1, 1)
    scaling = lax.rsqrt(row_squares / D + epsilon)
    normed = (column_block.astype(jnp.float32) * scaling * gain_full).astype(jnp.bfloat16)
    normed_local = (own_block.astype(jnp.float32) * scaling * gain_local).astype(jnp.bfloat16)
    weight_cols = w_gate.shape[2]
    both_weights = jnp.concatenate([w_gate[0], w_gate_q[0]], axis=1)
    both_acc = jnp.dot(normed, both_weights, preferred_element_type=jnp.float32)
    full_acc = both_acc[:, :weight_cols]
    quant_acc = both_acc[:, weight_cols:]
    block_squares = jnp.einsum("rc,rc->c", normed_local, normed_local, preferred_element_type=jnp.float32)
    total_load = jnp.sum(arrived_counts)
    hess_local = 2.0 * block_squares / total_load
    difference = full_acc - quant_acc
    err_part = jnp.sum(difference * difference, axis=1) / FF
    pow_part = jnp.sum(full_acc * full_acc, axis=1) / FF
    partial = jnp.concatenate([err_part, pow_part]).reshape(-1, 128)
    (gathered,) = exchange([(partial, True)], "tensor", 2, n_tensor)
    slots = jnp.sum(gathered, axis=0).reshape(2, n_expert, CAP).transpose(1, 0, 2)
    expert_total = jnp.sum(slots[:, 0]) / (jnp.sum(slots[:, 1]) + epsilon)
    slot_ratios = (slots[:, 0] / (slots[:, 1] + epsilon)).reshape(n_expert, 1, CAP)
    (back,) = exchange([(slot_ratios, False)], "expert", 3, n_expert)
    ratios = jnp.take(back.reshape(-1), target).reshape(tok_count, top_count)
    token_error = jnp.sum(route_weights * ratios, axis=1)
    return (token_error, expert_total.reshape(1), hess_local.reshape(1, local_cols))


def solution(mesh):
    placed = (
        P("expert", "tensor"),
        P("tensor", "expert", None),
        P("tensor"),
        P("expert", None),
        P("expert", None),
        P("expert", None, "tensor"),
        P("expert", None, "tensor"),
    )
    return jax.shard_map(
        per_device,
        mesh=mesh,
        in_specs=placed,
        out_specs=(P("expert"), P("expert"), P("expert", "tensor")),
        check_vma=False,
    )
```

```python
import jax
import jax.numpy as jnp
from jax import lax
from jax.experimental import pallas as pl
from jax.experimental.pallas import tpu as pltpu
from jax.sharding import PartitionSpec as P

D = 7168
FF = 2048
CAP = 24


epsilon = 1e-06

MESH_ID = pl.DeviceIdType.MESH


def exchange(arrays, axis, cid, size, stride=1):
    count = len(arrays)
    modes = [gather for _, gather in arrays]

    def kernel(*refs):
        x_refs = refs[:count]
        o_refs = refs[count:2 * count]
        local_sem, send_sem, recv_sem = refs[2 * count:]
        me = lax.axis_index(axis)
        pos = lax.rem(lax.div(me, stride), size)
        base = me - pos * stride

        def member(k):
            return base + lax.rem(pos + k, size) * stride

        barrier = pltpu.get_barrier_semaphore()
        for k in range(1, size):
            pl.semaphore_signal(barrier, inc=1, device_id={axis: member(k)}, device_id_type=MESH_ID)
        pl.semaphore_wait(barrier, size - 1)
        copies = []
        for a in range(count):
            x_ref, o_ref, gather = x_refs[a], o_refs[a], modes[a]
            local = pltpu.make_async_copy(x_ref if gather else x_ref.at[pos], o_ref.at[pos], local_sem.at[a])
            local.start()
            copies.append(local)
        for k in range(1, size):
            peer_pos = lax.rem(pos + k, size)
            for a in range(count):
                x_ref, o_ref, gather = x_refs[a], o_refs[a], modes[a]
                copy = pltpu.make_async_remote_copy(
                    src_ref=x_ref if gather else x_ref.at[peer_pos],
                    dst_ref=o_ref.at[pos],
                    send_sem=send_sem.at[a, k],
                    recv_sem=recv_sem.at[a, k],
                    device_id={axis: member(k)},
                    device_id_type=MESH_ID,
                )
                copy.start()
                copies.append(copy)
        for copy in copies:
            copy.wait()

    out_shape = [
        jax.ShapeDtypeStruct((size,) + tuple(x.shape if gather else x.shape[1:]), x.dtype)
        for x, gather in arrays
    ]
    return pl.pallas_call(
        kernel,
        out_shape=out_shape,
        in_specs=[pl.BlockSpec(memory_space=pltpu.VMEM)] * count,
        out_specs=[pl.BlockSpec(memory_space=pltpu.VMEM)] * count,
        scratch_shapes=[
            pltpu.SemaphoreType.DMA((count,)),
            pltpu.SemaphoreType.DMA((count, size)),
            pltpu.SemaphoreType.DMA((count, size)),
        ],
        compiler_params=pltpu.CompilerParams(collective_id=cid, has_side_effects=True),
    )(*[x for x, _ in arrays])


def per_device(residual, attn_parts, norm_gain, routes, route_weights, w_gate, w_gate_q):
    n_expert = lax.axis_size("expert")
    n_tensor = lax.axis_size("tensor")
    tok_count = residual.shape[0]
    local_cols = residual.shape[1]
    top_count = routes.shape[1]
    gain_local = norm_gain.astype(jnp.float32)[None, :]
    n_chip = n_tensor // 2
    dense_rows = tok_count * local_cols // 128
    column_parts = attn_parts[0].reshape(tok_count, n_chip, 2, local_cols).transpose(2, 1, 0, 3)
    column_parts = column_parts.reshape(2, n_chip, dense_rows, 128)
    pair_in, gain_pair = exchange([(column_parts, False), (norm_gain.reshape(1, local_cols), True)], "tensor", 0, 2)
    pair_sum = (pair_in[0].astype(jnp.float32) + pair_in[1].astype(jnp.float32)).astype(jnp.bfloat16)
    parts_in, gain_in = exchange([(pair_sum, False), (gain_pair, True)], "tensor", 4, n_chip, 2)
    gain_full = gain_in.reshape(1, n_tensor * local_cols).astype(jnp.float32)
    summed = jnp.sum(parts_in.astype(jnp.float32), axis=0).reshape(tok_count, local_cols)
    hidden = (residual.astype(jnp.float32) + summed).astype(jnp.bfloat16)
    expert_ids = jnp.arange(n_expert, dtype=jnp.int32)
    flat_routes = routes.reshape(-1)
    one_hot = (flat_routes[:, None] == expert_ids[None, :]).astype(jnp.int32)
    earlier = jnp.cumsum(one_hot, axis=0) - one_hot
    slot_index = jnp.sum(earlier * one_hot, axis=1)
    target = flat_routes * CAP + slot_index
    load_counts = jnp.sum(one_hot, axis=0)
    slot_ids = jnp.arange(n_expert * CAP, dtype=jnp.int32)
    placing = (slot_ids[:, None] == target[None, :]).reshape(n_expert * CAP, tok_count, top_count)
    dispatch = jnp.sum(placing.astype(jnp.int32), axis=2).astype(jnp.bfloat16)
    outgoing = jnp.dot(dispatch, hidden, preferred_element_type=jnp.float32).astype(jnp.bfloat16)
    lane_rows = CAP * local_cols // 128
    outgoing = outgoing.reshape(n_expert, lane_rows, 128)
    count_rows = jnp.broadcast_to(load_counts.astype(jnp.bfloat16)[:, None, None], (n_expert, 1, 128))
    outgoing = jnp.concatenate([outgoing, count_rows], axis=1)
    (arrived,) = exchange([(outgoing, False)], "expert", 1, n_expert)
    arrived_counts = arrived[:, lane_rows, 0].astype(jnp.float32)
    own_block = arrived[:, :lane_rows, :].reshape(n_expert * CAP, local_cols)
    column_block = lax.all_gather(own_block, "tensor", axis=1, tiled=True)
    own_wide = own_block.astype(jnp.float32)
    own_squares = jnp.sum(own_wide * own_wide, axis=1).reshape(-1, 128)
    (squares_in,) = exchange([(own_squares, True)], "tensor", 6, n_tensor)
    row_squares = jnp.sum(squares_in, axis=0).reshape(-1, 1)
    scaling = lax.rsqrt(row_squares / D + epsilon)
    normed = (column_block.astype(jnp.float32) * scaling * gain_full).astype(jnp.bfloat16)
    normed_local = (own_block.astype(jnp.float32) * scaling * gain_local).astype(jnp.bfloat16)
    weight_cols = w_gate.shape[2]
    both_weights = jnp.concatenate([w_gate[0], w_gate_q[0]], axis=1)
    both_acc = jnp.dot(normed, both_weights, preferred_element_type=jnp.float32)
    full_acc = both_acc[:, :weight_cols]
    quant_acc = both_acc[:, weight_cols:]
    block_squares = jnp.einsum("rc,rc->c", normed_local, normed_local, preferred_element_type=jnp.float32)
    total_load = jnp.sum(arrived_counts)
    hess_local = 2.0 * block_squares / total_load
    difference = full_acc - quant_acc
    err_part = jnp.sum(difference * difference, axis=1) / FF
    pow_part = jnp.sum(full_acc * full_acc, axis=1) / FF
    partial = jnp.concatenate([err_part, pow_part]).reshape(-1, 128)
    (gathered,) = exchange([(partial, True)], "tensor", 2, n_tensor)
    slots = jnp.sum(gathered, axis=0).reshape(2, n_expert, CAP).transpose(1, 0, 2)
    expert_total = jnp.sum(slots[:, 0]) / (jnp.sum(slots[:, 1]) + epsilon)
    slot_ratios = (slots[:, 0] / (slots[:, 1] + epsilon)).reshape(n_expert, 1, CAP)
    (back,) = exchange([(slot_ratios, False)], "expert", 3, n_expert)
    ratios = jnp.take(back.reshape(-1), target).reshape(tok_count, top_count)
    token_error = jnp.sum(route_weights * ratios, axis=1)
    return (token_error, expert_total.reshape(1), hess_local.reshape(1, local_cols))


def solution(mesh):
    placed = (
        P("expert", "tensor"),
        P("tensor", "expert", None),
        P("tensor"),
        P("expert", None),
        P("expert", None),
        P("expert", None, "tensor"),
        P("expert", None, "tensor"),
    )
    return jax.shard_map(
        per_device,
        mesh=mesh,
        in_specs=placed,
        out_specs=(P("expert"), P("expert"), P("expert", "tensor")),
        check_vma=False,
    )
```

```python
import jax
import jax.numpy as jnp
from jax import lax
from jax.experimental import pallas as pl
from jax.experimental.pallas import tpu as pltpu
from jax.sharding import PartitionSpec as P

D = 7168
FF = 2048
CAP = 24


epsilon = 1e-06

MESH_ID = pl.DeviceIdType.MESH


def exchange(arrays, axis, cid, size, stride=1):
    count = len(arrays)
    modes = [gather for _, gather in arrays]

    def kernel(*refs):
        x_refs = refs[:count]
        o_refs = refs[count:2 * count]
        local_sem, send_sem, recv_sem = refs[2 * count:]
        me = lax.axis_index(axis)
        pos = lax.rem(lax.div(me, stride), size)
        base = me - pos * stride

        def member(k):
            return base + lax.rem(pos + k, size) * stride

        barrier = pltpu.get_barrier_semaphore()
        for k in range(1, size):
            pl.semaphore_signal(barrier, inc=1, device_id={axis: member(k)}, device_id_type=MESH_ID)
        pl.semaphore_wait(barrier, size - 1)
        copies = []
        for a in range(count):
            x_ref, o_ref, gather = x_refs[a], o_refs[a], modes[a]
            local = pltpu.make_async_copy(x_ref if gather else x_ref.at[pos], o_ref.at[pos], local_sem.at[a])
            local.start()
            copies.append(local)
        for k in range(1, size):
            peer_pos = lax.rem(pos + k, size)
            for a in range(count):
                x_ref, o_ref, gather = x_refs[a], o_refs[a], modes[a]
                copy = pltpu.make_async_remote_copy(
                    src_ref=x_ref if gather else x_ref.at[peer_pos],
                    dst_ref=o_ref.at[pos],
                    send_sem=send_sem.at[a, k],
                    recv_sem=recv_sem.at[a, k],
                    device_id={axis: member(k)},
                    device_id_type=MESH_ID,
                )
                copy.start()
                copies.append(copy)
        for copy in copies:
            copy.wait()

    out_shape = [
        jax.ShapeDtypeStruct((size,) + tuple(x.shape if gather else x.shape[1:]), x.dtype)
        for x, gather in arrays
    ]
    return pl.pallas_call(
        kernel,
        out_shape=out_shape,
        in_specs=[pl.BlockSpec(memory_space=pltpu.VMEM)] * count,
        out_specs=[pl.BlockSpec(memory_space=pltpu.VMEM)] * count,
        scratch_shapes=[
            pltpu.SemaphoreType.DMA((count,)),
            pltpu.SemaphoreType.DMA((count, size)),
            pltpu.SemaphoreType.DMA((count, size)),
        ],
        compiler_params=pltpu.CompilerParams(collective_id=cid, has_side_effects=True),
    )(*[x for x, _ in arrays])


def per_device(residual, attn_parts, norm_gain, routes, route_weights, w_gate, w_gate_q):
    n_expert = lax.axis_size("expert")
    n_tensor = lax.axis_size("tensor")
    tok_count = residual.shape[0]
    local_cols = residual.shape[1]
    top_count = routes.shape[1]
    gain_local = norm_gain.astype(jnp.float32)[None, :]
    n_chip = n_tensor // 2
    column_parts = attn_parts[0].reshape(tok_count, n_chip, 2, local_cols).transpose(2, 1, 0, 3)
    pair_in, gain_pair = exchange([(column_parts, False), (norm_gain.reshape(1, local_cols), True)], "tensor", 0, 2)
    pair_sum = (pair_in[0].astype(jnp.float32) + pair_in[1].astype(jnp.float32)).astype(jnp.bfloat16)
    parts_in, gain_in = exchange([(pair_sum, False), (gain_pair, True)], "tensor", 4, n_chip, 2)
    gain_full = gain_in.reshape(1, n_tensor * local_cols).astype(jnp.float32)
    summed = jnp.sum(parts_in.astype(jnp.float32), axis=0)
    hidden = (residual.astype(jnp.float32) + summed).astype(jnp.bfloat16)
    expert_ids = jnp.arange(n_expert, dtype=jnp.int32)
    flat_routes = routes.reshape(-1)
    one_hot = (flat_routes[:, None] == expert_ids[None, :]).astype(jnp.int32)
    earlier = jnp.cumsum(one_hot, axis=0) - one_hot
    slot_index = jnp.sum(earlier * one_hot, axis=1)
    target = flat_routes * CAP + slot_index
    load_counts = jnp.sum(one_hot, axis=0)
    slot_ids = jnp.arange(n_expert * CAP, dtype=jnp.int32)
    placing = (slot_ids[:, None] == target[None, :]).reshape(n_expert * CAP, tok_count, top_count)
    dispatch = jnp.sum(placing.astype(jnp.int32), axis=2).astype(jnp.bfloat16)
    weighted_slots = jnp.sum(jnp.where(placing, route_weights[None, :, :], 0.0), axis=2)
    outgoing = jnp.dot(dispatch, hidden, preferred_element_type=jnp.float32).astype(jnp.bfloat16)
    lane_rows = CAP * local_cols // 128
    outgoing = outgoing.reshape(n_expert, lane_rows, 128)
    count_rows = jnp.broadcast_to(load_counts.astype(jnp.bfloat16)[:, None, None], (n_expert, 1, 128))
    outgoing = jnp.concatenate([outgoing, count_rows], axis=1)
    (arrived,) = exchange([(outgoing, False)], "expert", 1, n_expert)
    arrived_counts = arrived[:, lane_rows, 0].astype(jnp.float32)
    own_block = arrived[:, :lane_rows, :].reshape(n_expert * CAP, local_cols)
    column_block = lax.all_gather(own_block, "tensor", axis=1, tiled=True)
    own_wide = own_block.astype(jnp.float32)
    own_squares = jnp.sum(own_wide * own_wide, axis=1).reshape(-1, 128)
    (squares_in,) = exchange([(own_squares, True)], "tensor", 6, n_tensor)
    row_squares = jnp.sum(squares_in, axis=0).reshape(-1, 1)
    scaling = lax.rsqrt(row_squares / D + epsilon)
    normed = (column_block.astype(jnp.float32) * scaling * gain_full).astype(jnp.bfloat16)
    normed_local = (own_block.astype(jnp.float32) * scaling * gain_local).astype(jnp.bfloat16)
    weight_cols = w_gate.shape[2]
    both_weights = jnp.concatenate([w_gate[0], w_gate_q[0]], axis=1)
    both_acc = jnp.dot(normed, both_weights, preferred_element_type=jnp.float32)
    full_acc = both_acc[:, :weight_cols]
    quant_acc = both_acc[:, weight_cols:]
    block_squares = jnp.einsum("rc,rc->c", normed_local, normed_local, preferred_element_type=jnp.float32)
    total_load = jnp.sum(arrived_counts)
    hess_local = 2.0 * block_squares / total_load
    difference = full_acc - quant_acc
    err_part = jnp.sum(difference * difference, axis=1) / FF
    pow_part = jnp.sum(full_acc * full_acc, axis=1) / FF
    partial = jnp.concatenate([err_part, pow_part]).reshape(-1, 128)
    (gathered,) = exchange([(partial, True)], "tensor", 2, n_tensor)
    slots = jnp.sum(gathered, axis=0).reshape(2, n_expert, CAP).transpose(1, 0, 2)
    expert_total = jnp.sum(slots[:, 0]) / (jnp.sum(slots[:, 1]) + epsilon)
    slot_ratios = (slots[:, 0] / (slots[:, 1] + epsilon)).reshape(n_expert, 1, CAP)
    (back,) = exchange([(slot_ratios, False)], "expert", 3, n_expert)
    token_error = jnp.dot(back.reshape(1, -1), weighted_slots, precision=lax.Precision.HIGHEST).reshape(tok_count)
    return (token_error, expert_total.reshape(1), hess_local.reshape(1, local_cols))


def solution(mesh):
    placed = (
        P("expert", "tensor"),
        P("tensor", "expert", None),
        P("tensor"),
        P("expert", None),
        P("expert", None),
        P("expert", None, "tensor"),
        P("expert", None, "tensor"),
    )
    return jax.shard_map(
        per_device,
        mesh=mesh,
        in_specs=placed,
        out_specs=(P("expert"), P("expert"), P("expert", "tensor")),
        check_vma=False,
    )
```

```python
import jax
import jax.numpy as jnp
from jax import lax
from jax.experimental import pallas as pl
from jax.experimental.pallas import tpu as pltpu
from jax.sharding import PartitionSpec as P

D = 7168
FF = 2048
CAP = 24


epsilon = 1e-06

MESH_ID = pl.DeviceIdType.MESH


def exchange(arrays, axis, cid, size, stride=1):
    count = len(arrays)
    modes = [gather for _, gather in arrays]

    def kernel(*refs):
        x_refs = refs[:count]
        o_refs = refs[count:2 * count]
        local_sem, send_sem, recv_sem = refs[2 * count:]
        me = lax.axis_index(axis)
        pos = lax.rem(lax.div(me, stride), size)
        base = me - pos * stride

        def member(k):
            return base + lax.rem(pos + k, size) * stride

        barrier = pltpu.get_barrier_semaphore()
        for k in range(1, size):
            pl.semaphore_signal(barrier, inc=1, device_id={axis: member(k)}, device_id_type=MESH_ID)
        pl.semaphore_wait(barrier, size - 1)
        copies = []
        for a in range(count):
            x_ref, o_ref, gather = x_refs[a], o_refs[a], modes[a]
            local = pltpu.make_async_copy(x_ref if gather else x_ref.at[pos], o_ref.at[pos], local_sem.at[a])
            local.start()
            copies.append(local)
        for k in range(1, size):
            peer_pos = lax.rem(pos + k, size)
            for a in range(count):
                x_ref, o_ref, gather = x_refs[a], o_refs[a], modes[a]
                copy = pltpu.make_async_remote_copy(
                    src_ref=x_ref if gather else x_ref.at[peer_pos],
                    dst_ref=o_ref.at[pos],
                    send_sem=send_sem.at[a, k],
                    recv_sem=recv_sem.at[a, k],
                    device_id={axis: member(k)},
                    device_id_type=MESH_ID,
                )
                copy.start()
                copies.append(copy)
        for copy in copies:
            copy.wait()

    out_shape = [
        jax.ShapeDtypeStruct((size,) + tuple(x.shape if gather else x.shape[1:]), x.dtype)
        for x, gather in arrays
    ]
    return pl.pallas_call(
        kernel,
        out_shape=out_shape,
        in_specs=[pl.BlockSpec(memory_space=pltpu.VMEM)] * count,
        out_specs=[pl.BlockSpec(memory_space=pltpu.VMEM)] * count,
        scratch_shapes=[
            pltpu.SemaphoreType.DMA((count,)),
            pltpu.SemaphoreType.DMA((count, size)),
            pltpu.SemaphoreType.DMA((count, size)),
        ],
        compiler_params=pltpu.CompilerParams(collective_id=cid, has_side_effects=True),
    )(*[x for x, _ in arrays])


def per_device(residual, attn_parts, norm_gain, routes, route_weights, w_gate, w_gate_q):
    n_expert = lax.axis_size("expert")
    n_tensor = lax.axis_size("tensor")
    tok_count = residual.shape[0]
    local_cols = residual.shape[1]
    top_count = routes.shape[1]
    gain_local = norm_gain.astype(jnp.float32)[None, :]
    n_chip = n_tensor // 2
    column_parts = attn_parts[0].reshape(tok_count, n_chip, 2, local_cols).transpose(2, 1, 0, 3)
    pair_in, gain_pair = exchange([(column_parts, False), (norm_gain.reshape(1, local_cols), True)], "tensor", 0, 2)
    pair_sum = (pair_in[0].astype(jnp.float32) + pair_in[1].astype(jnp.float32)).astype(jnp.bfloat16)
    parts_in, gain_in = exchange([(pair_sum, False), (gain_pair, True)], "tensor", 4, n_chip, 2)
    gain_full = gain_in.reshape(1, n_tensor * local_cols).astype(jnp.float32)
    summed = jnp.sum(parts_in.astype(jnp.float32), axis=0)
    hidden = (residual.astype(jnp.float32) + summed).astype(jnp.bfloat16)
    expert_ids = jnp.arange(n_expert, dtype=jnp.int32)
    flat_routes = routes.reshape(-1)
    one_hot = (flat_routes[:, None] == expert_ids[None, :]).astype(jnp.int32)
    earlier = jnp.cumsum(one_hot, axis=0) - one_hot
    slot_index = jnp.sum(earlier * one_hot, axis=1)
    target = flat_routes * CAP + slot_index
    load_counts = jnp.sum(one_hot, axis=0)
    slot_ids = jnp.arange(n_expert * CAP, dtype=jnp.int32)
    placing = (slot_ids[:, None] == target[None, :]).reshape(n_expert * CAP, tok_count, top_count)
    dispatch = jnp.sum(placing.astype(jnp.int32), axis=2).astype(jnp.bfloat16)
    weighted_slots = jnp.sum(jnp.where(placing, route_weights[None, :, :], 0.0), axis=2)
    outgoing = jnp.dot(dispatch, hidden, preferred_element_type=jnp.float32).astype(jnp.bfloat16)
    lane_rows = CAP * local_cols // 128
    outgoing = outgoing.reshape(n_expert, lane_rows, 128)
    count_rows = jnp.broadcast_to(load_counts.astype(jnp.bfloat16)[:, None, None], (n_expert, 1, 128))
    outgoing = jnp.concatenate([outgoing, count_rows], axis=1)
    (arrived,) = exchange([(outgoing, False)], "expert", 1, n_expert)
    arrived_counts = arrived[:, lane_rows, 0].astype(jnp.float32)
    own_block = arrived[:, :lane_rows, :].reshape(n_expert * CAP, local_cols)
    column_block = lax.all_gather(own_block, "tensor", axis=1, tiled=True)
    own_wide = own_block.astype(jnp.float32)
    own_squares = jnp.sum(own_wide * own_wide, axis=1).reshape(-1, 128)
    (squares_in,) = exchange([(own_squares, True)], "tensor", 6, n_tensor)
    row_squares = jnp.sum(squares_in, axis=0).reshape(-1, 1)
    scaling = lax.rsqrt(row_squares / D + epsilon)
    normed = (column_block.astype(jnp.float32) * scaling * gain_full).astype(jnp.bfloat16)
    normed_local = (own_block.astype(jnp.float32) * scaling * gain_local).astype(jnp.bfloat16)
    weight_cols = w_gate.shape[2]
    both_weights = jnp.concatenate([w_gate[0], w_gate_q[0]], axis=1)
    both_acc = jnp.dot(normed, both_weights, preferred_element_type=jnp.float32)
    full_acc = both_acc[:, :weight_cols]
    quant_acc = both_acc[:, weight_cols:]
    block_squares = jnp.einsum("rc,rc->c", normed_local, normed_local, preferred_element_type=jnp.float32)
    total_load = jnp.sum(arrived_counts)
    hess_local = 2.0 * block_squares / total_load
    difference = full_acc - quant_acc
    err_part = jnp.sum(difference * difference, axis=1) / FF
    pow_part = jnp.sum(full_acc * full_acc, axis=1) / FF
    partial = jnp.concatenate([err_part, pow_part]).reshape(-1, 128)
    (gathered,) = exchange([(partial, True)], "tensor", 2, n_tensor)
    slots = jnp.sum(gathered, axis=0)
    half = slots.shape[0] // 2
    expert_total = jnp.sum(slots[:half]) / (jnp.sum(slots[half:]) + epsilon)
    slot_ratios = (slots[:half] / (slots[half:] + epsilon)).reshape(n_expert, 1, CAP)
    (back,) = exchange([(slot_ratios, False)], "expert", 3, n_expert)
    token_error = jnp.dot(back.reshape(1, -1), weighted_slots, precision=lax.Precision.HIGHEST).reshape(tok_count)
    return (token_error, expert_total.reshape(1), hess_local.reshape(1, local_cols))


def solution(mesh):
    placed = (
        P("expert", "tensor"),
        P("tensor", "expert", None),
        P("tensor"),
        P("expert", None),
        P("expert", None),
        P("expert", None, "tensor"),
        P("expert", None, "tensor"),
    )
    return jax.shard_map(
        per_device,
        mesh=mesh,
        in_specs=placed,
        out_specs=(P("expert"), P("expert"), P("expert", "tensor")),
        check_vma=False,
    )
```
